512 devices in a mesh: row: 32 (over z_lo, y), col: 16 (over z_hi, x, core).
Axes of the slice: x: 4, y: 4, z: 16 (z_hi: 2, z_lo: 8; z = z_hi * 8 + z_lo), core: 2. Of those that a mesh axis runs over, the one named last changes fastest.
Arguments:
- prefill_hidden: bfloat16 [4, 2048, 2880], P(None, 'row', 'col'), may hold values from -6 to 6
- decode_hidden: bfloat16 [128, 2880], P('row', 'col'), may hold values from -6 to 6
- norm_gain: bfloat16 [2880], replicated, may hold values from 0.5 to 1.5
- query_weight: bfloat16 [2880, 4096], P('row', 'col'), may hold values from -0.11388673 to 0.11388673
- kv_weight: bfloat16 [2880, 2, 512], P('row'), may hold values from -0.11388673 to 0.11388673
- out_weight: bfloat16 [4096, 2880], P('col', 'row'), may hold values from -0.09375 to 0.09375
- sink_logits: bfloat16 [64], P('col'), may hold values from -4 to 4
- key_pool: bfloat16 [768, 64, 512], P('row'), may hold values from -6 to 6
- value_pool: bfloat16 [768, 64, 512], P('row'), may hold values from -6 to 6
- lengths: int32 [32, 4], P('row'), may hold values from 1 to 384, 960 in all within a row
- page_table: int32 [32, 24], P('row'), may hold values from 0 to 23, each once within a row
Outputs:
- prefill_out: bfloat16 [4, 2048, 2880], P(None, 'row', 'col')
- decode_out: bfloat16 [128, 2880], P('row', 'col')
The draws below stay inside these ranges and needn't reach their ends.
Inputs may be any that keep to these rules, and one draw needn't show every extreme that they name: The 4 cached lengths of one index of row sum to 960, and some request has length 384. `page_table`: each line lists every local page of one index of row exactly once; request r % 4 of that index owns entries (r % 4) * 6 to (r % 4 + 1) * 6 - 1.
All inputs are finite; a program needn't handle non-finite values.
Results may differ from the reference program's by a relative error of at most 0.012.
Values may be sent and summed in bfloat16 or wider, within the bound.
A program may use at most 64 MiB of HBM per device.

```python
import math
import jax
import jax.numpy as jnp
import numpy as np
from jax import lax

D = 2880
HQ = 64
KV = 8
HD = 64
NPRE = 4
DEC_DEV = 4
MAXLEN = 384
PAGE = 64
MAXPAGES = 6
PLEN = 2048
NDEC = 128
POOL_DEV = 24
POOL = 768
N_ROW = 32


def drawn_rows(key, shape):
    base = jax.random.truncated_normal(jax.random.fold_in(key, 1), -6.0, 6.0, shape, jnp.float32)
    return base


def draw_prefill_hidden(key, part):
    return drawn_rows(key, (NPRE, PLEN, D)).astype(jnp.bfloat16)


def draw_decode_hidden(key, part):
    return drawn_rows(key, (NDEC, D)).astype(jnp.bfloat16)


def draw_query_weight(key, part):
    base = jax.random.truncated_normal(jax.random.fold_in(key, 11), -6.0, 6.0, (D, HQ * HD), jnp.float32) / math.sqrt(D)
    return base.astype(jnp.bfloat16)


def draw_kv_weight(key, part):
    base = jax.random.truncated_normal(jax.random.fold_in(key, 21), -6.0, 6.0, (D, 2, KV * HD), jnp.float32) / math.sqrt(D)
    return base.astype(jnp.bfloat16)


def draw_key_pool(key, part):
    base = jax.random.truncated_normal(jax.random.fold_in(key, 31), -6.0, 6.0, (POOL, PAGE, KV * HD), jnp.float32)
    return base.astype(jnp.bfloat16)


def block_scale(rng, dims, cuts, smallest, high):
    def one(position, blocks):
        heights = jax.random.uniform(jax.random.fold_in(jax.random.fold_in(rng, 6), position), (blocks,), jnp.float32, smallest / len(cuts), high / len(cuts))
        return jnp.repeat(jnp.exp(heights), dims[position] // blocks).reshape((-1,) + (1,) * (len(dims) - position - 1))

    level = one(*cuts[0])
    for cut in cuts[1:]:
        level = level * one(*cut)
    return level


def split_up(count, total, reach, slope):
    portions = [(1 << 20) // math.isqrt(rank ** slope) + 1 for rank in range(2, count + 1)]
    spare, given = total - reach - (count - 1), [1] * (count - 1)
    while spare > 0:
        candidates = [i for i in range(count - 1) if given[i] < reach]
        pool, remaining = sum([portions[i] for i in candidates]), spare
        for i in candidates:
            addition = min(reach - given[i], max(1, remaining * portions[i] // pool), spare)
            given[i] = given[i] + addition
            spare = spare - addition
    return np.array([reach] + given)


def ragged_sizes(key, number_of, total, reach, skew):
    if number_of == 2:
        one = jax.random.randint(key, (), max(1, total - reach), min(reach, total - 1) + 1)
        return jnp.stack([one, total - one])
    tallies = jnp.asarray(split_up(number_of, total, reach, skew), jnp.int32)
    couples = (number_of - 1) // 2
    giver, taker = tallies[1:1 + 2 * couples:2], tallies[2:2 + 2 * couples:2]
    room = jnp.minimum(giver - 1, reach - taker)
    moved = jax.random.randint(jax.random.fold_in(key, 1), (couples,), 0, 1 << 20) % (room + 1)
    tallies = tallies.at[1:1 + 2 * couples:2].set(giver - moved).at[2:2 + 2 * couples:2].set(taker + moved)
    return tallies[jax.random.permutation(jax.random.fold_in(key, 2), number_of)]


def bell_draw(stream_key, shape, scale, most, split=(), held_as=jnp.bfloat16):
    array = scale * jax.random.normal(stream_key, shape, jnp.float32)
    if split:
        array = array * block_scale(stream_key, shape, split, -0.22, 0.18)
    return jnp.clip(array, -most, most).astype(held_as)


def setup_inputs(seed: int = 0) -> dict:
    keys = jax.random.split(jax.random.key(seed), 12)
    return {
        "prefill_hidden": draw_prefill_hidden(jax.random.fold_in(keys[11], 71), 0),
        "decode_hidden": draw_decode_hidden(jax.random.fold_in(keys[11], 71), 0),
        "norm_gain": jnp.clip(1.0 + 0.1 * jax.random.normal(keys[2], (D,), jnp.float32), 0.5, 1.5).astype(jnp.bfloat16),
        "query_weight": draw_query_weight(jax.random.fold_in(keys[11], 71), 0),
        "kv_weight": draw_kv_weight(jax.random.fold_in(keys[11], 71), 0),
        "out_weight": bell_draw(keys[5], (HQ * HD, D), (HQ * HD) ** -0.5, 0.09375, ((0, 16), (1, 32))),
        "sink_logits": bell_draw(keys[6], (HQ,), 1.0, 4.0, ((0, 16),)),
        "key_pool": draw_key_pool(jax.random.fold_in(keys[11], 71), 0),
        "value_pool": bell_draw(keys[8], (POOL, PAGE, KV * HD), 1.0, 6.0, ((0, 32),)),
        "lengths": jax.vmap(lambda own: ragged_sizes(own, DEC_DEV, DEC_DEV * MAXLEN * 5 // 8, MAXLEN, 2))(jax.random.split(keys[9], N_ROW)).reshape((N_ROW, DEC_DEV)).astype(jnp.int32),
        "page_table": jax.vmap(lambda own: jax.random.permutation(own, DEC_DEV * MAXPAGES))(jax.random.split(keys[10], N_ROW)).reshape((N_ROW, DEC_DEV * MAXPAGES)).astype(jnp.int32),
    }


def normed(token_rows, norm_gain):
    widened = token_rows.astype(jnp.float32)
    inverse = lax.rsqrt(lax.optimization_barrier(jnp.mean(widened * widened, axis=-1, keepdims=True)) + 1e-05)
    return (widened * inverse * norm_gain.astype(jnp.float32)).astype(jnp.bfloat16)

def reference(prefill_hidden, decode_hidden, norm_gain, query_weight, kv_weight, out_weight, sink_logits, key_pool, value_pool, lengths, page_table):
    score_scale = 1.0 / math.sqrt(HD)
    group_size = HQ // KV
    prefill_rows = prefill_hidden.reshape(NPRE * PLEN, D)

    def project(hidden):
        queries = jnp.dot(hidden, query_weight, preferred_element_type=jnp.float32).astype(jnp.bfloat16)
        key_rows = jnp.dot(hidden, kv_weight[:, 0, :], preferred_element_type=jnp.float32).astype(jnp.bfloat16)
        value_rows = jnp.dot(hidden, kv_weight[:, 1, :], preferred_element_type=jnp.float32).astype(jnp.bfloat16)
        return (queries, key_rows, value_rows)
    query_pre, key_pre, value_pre = project(normed(prefill_rows, norm_gain))
    query_heads = query_pre.reshape(NPRE, PLEN, HQ, HD).transpose(2, 0, 1, 3)
    key_heads = key_pre.reshape(NPRE, PLEN, KV, HD).transpose(2, 0, 1, 3)
    value_heads = value_pre.reshape(NPRE, PLEN, KV, HD).transpose(2, 0, 1, 3)
    causal = jnp.arange(PLEN)[None, :] <= jnp.arange(PLEN)[:, None]

    def one_head(item):
        query_one, sink_one, head_index = item
        key_one = lax.dynamic_index_in_dim(key_heads, head_index // group_size, 0, keepdims=False)
        value_one = lax.dynamic_index_in_dim(value_heads, head_index // group_size, 0, keepdims=False)
        scores = jnp.einsum('nqd,npd->nqp', query_one.astype(jnp.float32), key_one.astype(jnp.float32)) * score_scale
        scores = jnp.where(causal[None], scores, -jnp.inf)
        highest = jnp.maximum(lax.optimization_barrier(jnp.max(scores, axis=-1)), sink_one)
        weights = jnp.exp(scores - highest[..., None])
        denominator = lax.optimization_barrier(jnp.sum(weights, axis=-1)) + jnp.exp(sink_one - highest)
        summed = jnp.einsum('nqp,npd->nqd', weights.astype(jnp.bfloat16).astype(jnp.float32), value_one.astype(jnp.float32))
        return (summed / denominator[..., None]).astype(jnp.bfloat16)
    sink_all = sink_logits.astype(jnp.float32)
    head_out = lax.map(one_head, (query_heads, sink_all, jnp.arange(HQ, dtype=jnp.int32)))
    prefill_att = head_out.transpose(1, 2, 0, 3).reshape(NPRE * PLEN, HQ * HD)
    query_dec, key_dec, value_dec = project(normed(decode_hidden, norm_gain))
    owner_row = jnp.arange(NDEC, dtype=jnp.int32) // DEC_DEV
    global_pages = page_table.reshape(NDEC, MAXPAGES) + (owner_row * POOL_DEV)[:, None]
    key_cache = key_pool[global_pages].reshape(NDEC, MAXLEN, KV, HD).astype(jnp.float32)
    value_cache = value_pool[global_pages].reshape(NDEC, MAXLEN, KV, HD).astype(jnp.float32)
    query_grid = query_dec.reshape(NDEC, KV, group_size, HD).astype(jnp.float32)
    cache_scores = jnp.einsum('nkgd,ntkd->nkgt', query_grid, key_cache) * score_scale
    live = jnp.arange(MAXLEN, dtype=jnp.int32)[None, :] < lengths.reshape(NDEC)[:, None]
    cache_scores = jnp.where(live[:, None, None, :], cache_scores, -jnp.inf)
    self_scores = jnp.einsum('nkgd,nkd->nkg', query_grid, key_dec.reshape(NDEC, KV, HD).astype(jnp.float32)) * score_scale
    sink_grid = sink_all.reshape(KV, group_size)[None]
    highest = jnp.maximum(jnp.maximum(lax.optimization_barrier(jnp.max(cache_scores, axis=-1)), self_scores), sink_grid)
    cache_probs = jnp.exp(cache_scores - highest[..., None])
    self_probs = jnp.exp(self_scores - highest)
    denominator = lax.optimization_barrier(jnp.sum(cache_probs, axis=-1)) + self_probs + jnp.exp(sink_grid - highest)
    decode_sum = jnp.einsum('nkgt,ntkd->nkgd', cache_probs.astype(jnp.bfloat16).astype(jnp.float32), value_cache)
    decode_sum = decode_sum + self_probs.astype(jnp.bfloat16).astype(jnp.float32)[..., None] * value_dec.reshape(NDEC, KV, HD).astype(jnp.float32)[:, :, None, :]
    decode_att = (decode_sum / denominator[..., None]).reshape(NDEC, HQ * HD).astype(jnp.bfloat16)
    attended = jnp.concatenate([prefill_att, decode_att], axis=0)
    attn = jnp.dot(attended, out_weight, preferred_element_type=jnp.float32)
    residual = jnp.concatenate([prefill_rows, decode_hidden], axis=0).astype(jnp.float32)
    result = (residual + attn).astype(jnp.bfloat16)
    return (result[:NPRE * PLEN].reshape(NPRE, PLEN, D), result[NPRE * PLEN:])
```

```python
import math

import jax
import jax.numpy as jnp
from jax import lax
from jax.experimental import pallas as pl
from jax.experimental.pallas import tpu as pltpu
from jax.sharding import PartitionSpec as P

HQ = 64
KV = 8
HD = 64
ZL = 8
YN = 4
XN = 4
TOK = 272
HALF = TOK // 2
FOLD = TOK + HALF
FEAT = 192
MESH = pl.DeviceIdType.MESH
ROW_COPIES = 64
COL_COPIES = 24


def fold(rows):
    tail = jnp.concatenate([rows[:HALF, 128:FEAT], rows[HALF:, 128:FEAT]], axis=1)
    return jnp.concatenate([rows[:, :128], tail], axis=0)


def unfold(folded):
    head, tail = folded[..., :TOK, :], folded[..., TOK:, :]
    tail = jnp.concatenate([tail[..., :64], tail[..., 64:]], axis=-2)
    return jnp.concatenate([head, tail], axis=-1)


class Sender:
    def __init__(self, send_sem, recv_sem):
        self.send_sem, self.recv_sem = send_sem, recv_sem
        self.started = []

    def copy(self, index, src, dst, device):
        return pltpu.make_async_remote_copy(
            src_ref=src(),
            dst_ref=dst(),
            send_sem=self.send_sem.at[index],
            recv_sem=self.recv_sem.at[index],
            device_id=device,
            device_id_type=MESH,
        )

    def run(self, cond, action):
        if cond is None:
            action()
        else:
            pl.when(cond)(action)

    def send(self, index, src, dst, device, cond=None):
        self.run(cond, lambda: self.copy(index, src, dst, device).start())
        self.started.append((index, src, dst, device, cond))

    def arrive(self, index, slot, device, cond=None):
        self.run(cond, lambda: self.copy(index, slot, slot, device).wait_recv())

    def finish(self):
        for index, src, dst, device, cond in self.started:
            self.run(cond, lambda: self.copy(index, src, dst, device).wait_send())


def greet(pairs):
    barrier = pltpu.get_barrier_semaphore()
    for device, cond in pairs:
        def hello(device=device):
            pl.semaphore_signal(barrier, inc=1, device_id=device, device_id_type=MESH)

        if cond is None:
            hello()
        else:
            pl.when(cond)(hello)
    peers = sum(1 if cond is None else cond.astype(jnp.int32) for _, cond in pairs)
    pl.semaphore_wait(barrier, peers)


class RowGather:
    def __init__(self, block, out, send_sem, recv_sem):
        row, col = lax.axis_index("row"), lax.axis_index("col")
        self.row = row
        self.z, self.y = row // YN, lax.rem(row, YN)
        self.block, self.out = block, out
        self.up = (row + YN, col)
        self.down = (row - YN, col)
        self.has_up = self.z < ZL - 1
        self.has_down = self.z > 0
        self.after = (self.z * YN + lax.rem(self.y + 1, YN), col)
        self.before = (self.z * YN + lax.rem(self.y + YN - 1, YN), col)
        self.net = Sender(send_sem, recv_sem)

    def partners(self):
        return [
            (self.up, self.has_up),
            (self.down, self.has_down),
            (self.after, None),
            (self.before, None),
        ]

    def slot(self, z, shift):
        return lambda: self.out.at[z * YN + lax.rem(self.y + shift + YN, YN)]

    def events(self, distance):
        events = [(0, self.z - distance, self.z - distance >= 0)]
        if distance > 0:
            events.append((1, self.z + distance, self.z + distance < ZL))
        return events

    def along_z(self, distance):
        for way, z, exists in self.events(distance):
            mine = self.slot(z, 0)
            src = mine
            if distance == 0:
                src = lambda: self.block
            else:
                self.net.arrive(way * 8 + distance, mine, self.down if way == 0 else self.up, exists)
            if distance < ZL - 1:
                if way == 0:
                    self.net.send(
                        distance + 1, src, mine, self.up, jnp.logical_and(exists, self.has_up)
                    )
                if way == 1 or distance == 0:
                    self.net.send(
                        8 + distance + 1, src, mine, self.down, jnp.logical_and(exists, self.has_down)
                    )
            cond = None if distance == 0 else exists
            self.net.send(16 + way * 8 + distance, src, mine, self.after, cond)
            self.net.send(32 + way * 8 + distance, src, mine, self.before, cond)

    def along_y(self, distance):
        for way, z, exists in self.events(distance):
            cond = None if distance == 0 else exists
            index = way * 8 + distance
            self.net.arrive(16 + index, self.slot(z, -1), self.before, cond)
            if distance % 2 == 0:
                self.net.send(48 + index, self.slot(z, -1), self.slot(z, -1), self.after, cond)
            self.net.arrive(32 + index, self.slot(z, 1), self.after, cond)
            if distance % 2 == 1:
                self.net.send(48 + index, self.slot(z, 1), self.slot(z, 1), self.before, cond)

    def last(self):
        for distance in range(ZL):
            for way, z, exists in self.events(distance):
                cond = None if distance == 0 else exists
                source = self.before if distance % 2 == 0 else self.after
                self.net.arrive(48 + way * 8 + distance, self.slot(z, 2), source, cond)
        self.net.finish()


class ColGather:
    def __init__(self, block, out, send_sem, recv_sem):
        row, col = lax.axis_index("row"), lax.axis_index("col")
        self.high, self.x, self.core = col // (2 * XN), lax.rem(col // 2, XN), lax.rem(col, 2)
        self.block, self.out = block, out
        self.mate = (row, self.at(1, 0, 0))
        self.after = (row, self.at(0, 1, 0))
        self.before = (row, self.at(0, -1, 0))
        self.sibling = (row, self.at(0, 0, 1))
        self.net = Sender(send_sem, recv_sem)

    def partners(self):
        return [(self.mate, None), (self.after, None), (self.before, None), (self.sibling, None)]

    def at(self, high, shift, core):
        return (
            lax.rem(self.high + high, 2) * (2 * XN)
            + lax.rem(self.x + shift + XN, XN) * 2
            + lax.rem(self.core + core, 2)
        )

    def slot(self, high, shift, core=0):
        return lambda: self.out.at[self.at(high, shift, core)]

    def own(self, high):
        slot = self.slot(high, 0)
        src = slot
        if high == 0:
            src = lambda: self.block
            self.net.send(0, src, slot, self.mate)
        else:
            self.net.arrive(0, slot, self.mate)
        self.net.send(1 + high, src, slot, self.after)
        self.net.send(3 + high, src, slot, self.before)
        self.net.send(8 + high * 4, src, slot, self.sibling)

    def ring(self, high):
        self.net.arrive(1 + high, self.slot(high, -1), self.before)
        if high == 0:
            self.net.send(5, self.slot(high, -1), self.slot(high, -1), self.after)
        self.net.send(8 + high * 4 + 3, self.slot(high, -1), self.slot(high, -1), self.sibling)
        self.net.arrive(3 + high, self.slot(high, 1), self.after)
        if high == 1:
            self.net.send(6, self.slot(high, 1), self.slot(high, 1), self.before)
        self.net.send(8 + high * 4 + 1, self.slot(high, 1), self.slot(high, 1), self.sibling)

    def far(self, high):
        self.net.arrive(5 + high, self.slot(high, 2), self.before if high == 0 else self.after)
        self.net.send(8 + high * 4 + 2, self.slot(high, 2), self.slot(high, 2), self.sibling)

    def last(self):
        for high in range(2):
            for shift in range(XN):
                self.net.arrive(8 + high * 4 + shift, self.slot(high, shift, 1), self.sibling)
        self.net.finish()


def gather_kernel(
    weight_ref, token_ref, all_weight, all_token, rs, rr, cs, cr, local_sem
):
    rows = RowGather(weight_ref, all_weight, rs, rr)
    cols = ColGather(token_ref, all_token, cs, cr)
    greet(rows.partners() + cols.partners())
    cols.own(0)
    rows.along_z(0)
    own_weight = pltpu.make_async_copy(weight_ref, all_weight.at[rows.row], local_sem.at[0])
    own_token = pltpu.make_async_copy(
        token_ref, all_token.at[lax.axis_index("col")], local_sem.at[1]
    )
    own_weight.start()
    own_token.start()
    rows.along_z(1)
    rows.along_y(0)
    cols.ring(0)
    rows.along_z(2)
    rows.along_y(1)
    cols.own(1)
    rows.along_z(3)
    rows.along_y(2)
    cols.far(0)
    rows.along_z(4)
    rows.along_y(3)
    cols.ring(1)
    rows.along_z(5)
    rows.along_y(4)
    cols.far(1)
    rows.along_z(6)
    rows.along_y(5)
    rows.along_z(7)
    rows.along_y(6)
    rows.along_y(7)
    cols.last()
    rows.last()
    own_weight.wait()
    own_token.wait()


def vmem():
    return pl.BlockSpec(memory_space=pltpu.VMEM)


def gather_first(weight_block, token_block):
    return pl.pallas_call(
        gather_kernel,
        out_shape=(
            jax.ShapeDtypeStruct((ZL * YN,) + weight_block.shape, jnp.bfloat16),
            jax.ShapeDtypeStruct((4 * XN,) + token_block.shape, jnp.bfloat16),
        ),
        in_specs=[vmem()] * 2,
        out_specs=(vmem(), vmem()),
        scratch_shapes=[
            pltpu.SemaphoreType.DMA((ROW_COPIES,)),
            pltpu.SemaphoreType.DMA((ROW_COPIES,)),
            pltpu.SemaphoreType.DMA((COL_COPIES,)),
            pltpu.SemaphoreType.DMA((COL_COPIES,)),
            pltpu.SemaphoreType.DMA((2,)),
        ],
        compiler_params=pltpu.CompilerParams(
            collective_id=0, has_side_effects=True, vmem_limit_bytes=40 * 1024 * 1024
        ),
    )(weight_block, token_block)


def kv_kernel(block_ref, out_ref, send_sem, recv_sem, local_sem):
    rows = RowGather(block_ref, out_ref, send_sem, recv_sem)
    greet(rows.partners())
    rows.along_z(0)
    own = pltpu.make_async_copy(block_ref, out_ref.at[rows.row], local_sem.at[0])
    own.start()
    for distance in range(1, ZL):
        rows.along_z(distance)
        rows.along_y(distance - 1)
    rows.along_y(ZL - 1)
    rows.last()
    own.wait()


def gather_kv(block):
    return pl.pallas_call(
        kv_kernel,
        out_shape=jax.ShapeDtypeStruct((ZL * YN,) + block.shape, jnp.bfloat16),
        in_specs=[vmem()],
        out_specs=vmem(),
        scratch_shapes=[
            pltpu.SemaphoreType.DMA((ROW_COPIES,)),
            pltpu.SemaphoreType.DMA((ROW_COPIES,)),
            pltpu.SemaphoreType.DMA((1,)),
        ],
        compiler_params=pltpu.CompilerParams(
            collective_id=1, has_side_effects=True, vmem_limit_bytes=40 * 1024 * 1024
        ),
    )(block)


ORDER = ((1, 2), (0, 2), (1, 1), (1, 3), (0, 3), (0, 1), (1, 0), (0, 0))


def out_kernel(
    att_ref, weight_ref, token_ref, out_ref, first, landed, second, ring, keep, mate_out, mate_in,
    send_sem, recv_sem,
):
    row, col = lax.axis_index("row"), lax.axis_index("col")
    high, x, core = col // (2 * XN), lax.rem(col // 2, XN), lax.rem(col, 2)

    def at(dh, dx, dc):
        return (
            lax.rem(high + dh, 2) * (2 * XN) + lax.rem(x + dx + XN, XN) * 2 + lax.rem(core + dc, 2)
        )

    mate, after, before, sibling = (
        (row, at(1, 0, 0)), (row, at(0, 1, 0)), (row, at(0, -1, 0)), (row, at(0, 0, 1)),
    )
    greet([(mate, None), (after, None), (before, None), (sibling, None)])
    net = Sender(send_sem, recv_sem)

    def share(block):
        columns = pl.ds(384, 256)
        product = lax.dot_general(
            att_ref[...],
            weight_ref[block, :, columns],
            (((1,), (1,)), ((), ())),
            preferred_element_type=jnp.float32,
        )
        return fold(product)

    for k, (dh, dx) in enumerate(ORDER):
        first[k] = share(at(dh, dx, 1)).astype(jnp.bfloat16)
        net.send(k, lambda k=k: first.at[k], lambda k=k: landed.at[k], sibling)

    def summed(k):
        dh, dx = ORDER[k]
        own = share(at(dh, dx, 0))
        net.arrive(k, lambda: landed.at[k], sibling)
        return own + landed[k].astype(jnp.float32)

    def pass_on(index, value, device):
        second[index] = value.astype(jnp.bfloat16)
        net.send(8 + index, lambda: second.at[index], lambda: ring.at[index], device)

    def arrived(index, device):
        net.arrive(8 + index, lambda: ring.at[index], device)
        return ring[index].astype(jnp.float32)

    pass_on(0, summed(0), before)
    pass_on(1, summed(1), after)
    pass_on(2, summed(2), after)
    keep[0] = summed(3)
    pass_on(4, keep[0] + arrived(0, after), before)
    pass_on(3, summed(4), before)
    keep[1] = summed(5)
    pass_on(5, keep[1] + arrived(1, before), after)
    keep[2] = summed(6)
    mate_out[...] = (keep[2] + arrived(2, before) + arrived(4, after)).astype(jnp.bfloat16)
    net.send(14, lambda: mate_out, lambda: mate_in, mate)
    keep[3] = summed(7) + token_ref[...].astype(jnp.float32)
    total = keep[3] + arrived(3, after) + arrived(5, before)
    net.arrive(14, lambda: mate_in, mate)
    out_ref[...] = (total + mate_in[...].astype(jnp.float32)).astype(jnp.bfloat16)
    net.finish()


def project_out(att, weights, tokens):
    block = (FOLD, 128)
    return pl.pallas_call(
        out_kernel,
        out_shape=jax.ShapeDtypeStruct(block, jnp.bfloat16),
        in_specs=[vmem()] * 3,
        out_specs=vmem(),
        scratch_shapes=[
            pltpu.VMEM((8,) + block, jnp.bfloat16),
            pltpu.VMEM((8,) + block, jnp.bfloat16),
            pltpu.VMEM((6,) + block, jnp.bfloat16),
            pltpu.VMEM((6,) + block, jnp.bfloat16),
            pltpu.VMEM((4,) + block, jnp.float32),
            pltpu.VMEM(block, jnp.bfloat16),
            pltpu.VMEM(block, jnp.bfloat16),
            pltpu.SemaphoreType.DMA((16,)),
            pltpu.SemaphoreType.DMA((16,)),
        ],
        compiler_params=pltpu.CompilerParams(
            collective_id=2, has_side_effects=True, vmem_limit_bytes=40 * 1024 * 1024
        ),
    )(att, weights, tokens)


def normed(token_rows, norm_gain, count):
    widened = token_rows.astype(jnp.float32)
    mean = jnp.sum(widened * widened, axis=-1, keepdims=True) * (1.0 / count)
    inverse = lax.rsqrt(mean + 1e-05)
    return (widened * inverse * norm_gain.astype(jnp.float32)).astype(jnp.bfloat16)


def body(
    prefill_hidden,
    decode_hidden,
    norm_gain,
    query_weight,
    kv_weight,
    out_weight,
    sink_logits,
    key_pool,
    value_pool,
    lengths,
    page_table,
):
    spans, span_rows, col_width = prefill_hidden.shape
    decode_rows = decode_hidden.shape[0]
    prefill_count = spans * span_rows
    token_rows = jnp.concatenate(
        [prefill_hidden.reshape(prefill_count, col_width), decode_hidden], axis=0
    )
    heads_dev = query_weight.shape[1] // HD
    group_size = HQ // KV
    kv_dev = max(1, heads_dev // group_size)
    per_kv = heads_dev // kv_dev
    col_index = lax.axis_index("col")
    row_index = lax.axis_index("row")
    kv_first = col_index * heads_dev // group_size
    kv_columns = lax.dynamic_slice_in_dim(kv_weight, kv_first * HD, kv_dev * HD, 2).reshape(
        kv_weight.shape[0], 2 * kv_dev * HD
    )
    weight_block = jnp.concatenate([query_weight, kv_columns, out_weight.T], axis=1)
    weight_block = jnp.pad(weight_block, ((0, FEAT // 2 - weight_block.shape[0]), (0, 0)))
    token_wide = jnp.pad(
        token_rows.reshape(-1, 2, col_width // 2),
        ((0, TOK - token_rows.shape[0]), (0, 0), (0, FEAT // 2 - col_width // 2)),
    ).reshape(TOK, FEAT)
    token_block = fold(token_wide)
    all_weight, all_token = gather_first(weight_block, token_block)
    weights = all_weight.reshape(4 * XN, FEAT, weight_block.shape[1])
    features = unfold(all_token).transpose(1, 0, 2).reshape(TOK, 4 * XN * FEAT)
    gain = jnp.pad(
        norm_gain.reshape(-1, col_width // 2), ((0, 0), (0, FEAT // 2 - col_width // 2))
    ).reshape(4 * XN * FEAT)
    hidden = normed(features, gain, norm_gain.shape[0])
    qkv_sum = jnp.dot(
        hidden,
        weights.reshape(4 * XN * FEAT, -1)[:, : heads_dev * HD + 2 * kv_dev * HD],
        preferred_element_type=jnp.float32,
    )[: prefill_count + decode_rows]
    query_sum, kv_sum = qkv_sum[:, : heads_dev * HD], qkv_sum[:, heads_dev * HD :]
    queries = query_sum.astype(jnp.bfloat16)
    key_rows = kv_sum[:, : kv_dev * HD].astype(jnp.bfloat16)
    value_rows = kv_sum[:, kv_dev * HD :].astype(jnp.bfloat16)
    score_scale = 1.0 / math.sqrt(HD)
    sink_grid = sink_logits.astype(jnp.float32).reshape(kv_dev, per_kv)
    query_pre = queries[:prefill_count].reshape(spans, span_rows, kv_dev, per_kv, HD)
    positions = row_index * span_rows + jnp.arange(span_rows, dtype=jnp.int32)
    state_shape = (spans, kv_dev, per_kv, span_rows)
    kv_all = (
        gather_kv(kv_sum[:prefill_count].astype(jnp.bfloat16))
        .reshape(-1, spans, span_rows, 2 * kv_dev * HD)
        .transpose(1, 0, 2, 3)
        .reshape(spans, -1, 2 * kv_dev * HD)
    )
    pieces = (kv_all[..., : kv_dev * HD], kv_all[..., kv_dev * HD :])
    running = jnp.broadcast_to(sink_grid[None, :, :, None], state_shape)
    denominator = jnp.ones(state_shape, jnp.float32)
    weighted = jnp.zeros(state_shape + (HD,), jnp.float32)
    piece_len = pieces[0].shape[1]
    key_piece = pieces[0].reshape(spans, piece_len, kv_dev, HD)
    value_piece = pieces[1].reshape(spans, piece_len, kv_dev, HD)
    scores = (
        jnp.einsum("nqkgd,npkd->nkgqp", query_pre, key_piece, preferred_element_type=jnp.float32)
        * score_scale
    )
    key_pos = jnp.arange(piece_len, dtype=jnp.int32)
    allowed = key_pos[None, :] <= positions[:, None]
    scores = jnp.where(allowed, scores, -jnp.inf)
    newest = jnp.maximum(running, jnp.max(scores, axis=-1))
    probs_soft = jnp.exp(scores - newest[..., None])
    factor = jnp.exp(running - newest)
    denominator = denominator * factor + jnp.sum(probs_soft, axis=-1)
    weighted = weighted * factor[..., None] + jnp.einsum(
        "nkgqp,npkd->nkgqd",
        probs_soft.astype(jnp.bfloat16),
        value_piece,
        preferred_element_type=jnp.float32,
    )
    running, denominator, weighted = (newest, denominator, weighted)
    prefill_att = (
        (weighted / denominator[..., None])
        .transpose(0, 3, 1, 2, 4)
        .reshape(prefill_count, heads_dev * HD)
        .astype(jnp.bfloat16)
    )
    query_dec = queries[prefill_count:].reshape(decode_rows, kv_dev, per_kv, HD)
    key_new = key_rows[prefill_count:].reshape(decode_rows, kv_dev, HD)
    value_new = value_rows[prefill_count:].reshape(decode_rows, kv_dev, HD)
    pool_pages, page_len, pool_width = key_pool.shape
    table = page_table.reshape(decode_rows, -1)
    max_pages = table.shape[1]
    key_mine = lax.dynamic_slice_in_dim(
        key_pool.reshape(pool_pages, page_len, KV, HD), kv_first, kv_dev, 2
    )
    value_mine = lax.dynamic_slice_in_dim(
        value_pool.reshape(pool_pages, page_len, KV, HD), kv_first, kv_dev, 2
    )
    key_cache = key_mine[table].reshape(decode_rows, max_pages * page_len, kv_dev, HD)
    value_cache = value_mine[table].reshape(decode_rows, max_pages * page_len, kv_dev, HD)
    cache_scores = (
        jnp.einsum("skgd,stkd->skgt", query_dec, key_cache, preferred_element_type=jnp.float32)
        * score_scale
    )
    live = (
        jnp.arange(max_pages * page_len, dtype=jnp.int32)[None, :]
        < lengths.reshape(decode_rows)[:, None]
    )
    cache_scores = jnp.where(live[:, None, None, :], cache_scores, -jnp.inf)
    self_scores = (
        jnp.einsum("skgd,skd->skg", query_dec, key_new, preferred_element_type=jnp.float32)
        * score_scale
    )
    highest = jnp.maximum(jnp.maximum(jnp.max(cache_scores, axis=-1), self_scores), sink_grid[None])
    cache_probs = jnp.exp(cache_scores - highest[..., None])
    self_probs = jnp.exp(self_scores - highest)
    denom_dec = jnp.sum(cache_probs, axis=-1) + self_probs + jnp.exp(sink_grid[None] - highest)
    decode_sum = jnp.einsum(
        "skgt,stkd->skgd",
        cache_probs.astype(jnp.bfloat16),
        value_cache,
        preferred_element_type=jnp.float32,
    )
    decode_sum = (
        decode_sum
        + self_probs.astype(jnp.bfloat16).astype(jnp.float32)[..., None]
        * value_new.astype(jnp.float32)[:, :, None, :]
    )
    decode_att = (
        (decode_sum / denom_dec[..., None])
        .reshape(decode_rows, heads_dev * HD)
        .astype(jnp.bfloat16)
    )
    attended = jnp.concatenate([prefill_att, decode_att], axis=0)
    attended = jnp.pad(attended, ((0, TOK - attended.shape[0]), (0, 0)))
    folded = project_out(attended, weights, token_block)
    result = (
        unfold(folded)
        .reshape(TOK, 2, FEAT // 2)[: prefill_count + decode_rows, :, : col_width // 2]
        .reshape(-1, col_width)
    )
    return (result[:prefill_count].reshape(spans, span_rows, col_width), result[prefill_count:])


def solution(mesh):
    in_specs = (
        P(None, "row", "col"),
        P("row", "col"),
        P(),
        P("row", "col"),
        P("row", None, None),
        P("col", "row"),
        P("col"),
        P("row", None, None),
        P("row", None, None),
        P("row", None),
        P("row", None),
    )
    out_specs = (P(None, "row", "col"), P("row", "col"))
    return jax.shard_map(body, mesh=mesh, in_specs=in_specs, out_specs=out_specs, check_vma=False)
```

```python
import math

import jax
import jax.numpy as jnp
from jax import lax
from jax.experimental import pallas as pl
from jax.experimental.pallas import tpu as pltpu
from jax.sharding import PartitionSpec as P

HQ = 64
KV = 8
HD = 64
WIDTH = 2880
ZL = 8
YN = 4
XN = 4
TOK = 272
HALF = TOK // 2
FOLD = TOK + HALF
FEAT = 192
MESH = pl.DeviceIdType.MESH
ROW_COPIES = 64
SHARED_COPIES = 128
PIECE = FEAT // 2
Q_AT, O_AT, KV_AT = 0, 2 * PIECE, 4 * PIECE
BLOCK = 4 * PIECE + PIECE // 2
COL_COPIES = 24


def fold(rows):
    tail = jnp.concatenate([rows[:HALF, 128:FEAT], rows[HALF:, 128:FEAT]], axis=1)
    return jnp.concatenate([rows[:, :128], tail], axis=0)


def unfold(folded):
    head, tail = folded[..., :TOK, :], folded[..., TOK:, :]
    tail = jnp.concatenate([tail[..., :64], tail[..., 64:]], axis=-2)
    return jnp.concatenate([head, tail], axis=-1)


class Sender:
    def __init__(self, send_sem, recv_sem):
        self.send_sem, self.recv_sem = send_sem, recv_sem
        self.started = []

    def copy(self, index, src, dst, device):
        return pltpu.make_async_remote_copy(
            src_ref=src(),
            dst_ref=dst(),
            send_sem=self.send_sem.at[index],
            recv_sem=self.recv_sem.at[index],
            device_id=device,
            device_id_type=MESH,
        )

    def run(self, cond, action):
        if cond is None:
            action()
        else:
            pl.when(cond)(action)

    def send(self, index, src, dst, device, cond=None):
        self.run(cond, lambda: self.copy(index, src, dst, device).start())
        self.started.append((index, src, dst, device, cond))

    def arrive(self, index, slot, device, cond=None):
        self.run(cond, lambda: self.copy(index, slot, slot, device).wait_recv())

    def finish(self):
        for index, src, dst, device, cond in self.started:
            self.run(cond, lambda: self.copy(index, src, dst, device).wait_send())


def greet(pairs):
    barrier = pltpu.get_barrier_semaphore()
    for device, cond in pairs:
        def hello(device=device):
            pl.semaphore_signal(barrier, inc=1, device_id=device, device_id_type=MESH)

        if cond is None:
            hello()
        else:
            pl.when(cond)(hello)
    peers = sum(1 if cond is None else cond.astype(jnp.int32) for _, cond in pairs)
    pl.semaphore_wait(barrier, peers)


class RowGather:
    def __init__(self, block, out, send_sem, recv_sem, other=None):
        row, col = lax.axis_index("row"), lax.axis_index("col")
        self.row = row
        self.other = other
        self.sibling = (row, col + 1 - 2 * lax.rem(col, 2))
        self.z, self.y = row // YN, lax.rem(row, YN)
        self.block, self.out = block, out
        self.up = (row + YN, col)
        self.down = (row - YN, col)
        self.has_up = self.z < ZL - 1
        self.has_down = self.z > 0
        self.after = (self.z * YN + lax.rem(self.y + 1, YN), col)
        self.before = (self.z * YN + lax.rem(self.y + YN - 1, YN), col)
        self.net = Sender(send_sem, recv_sem)

    def partners(self):
        return [
            (self.up, self.has_up),
            (self.down, self.has_down),
            (self.after, None),
            (self.before, None),
        ]

    def slot(self, z, shift):
        return lambda: self.out(z * YN + lax.rem(self.y + shift + YN, YN))

    def share(self, index, src, z, shift, cond):
        if self.other is not None:
            self.net.send(64 + index, src, self.slot(z, shift), self.sibling, cond)

    def events(self, distance):
        events = [(0, self.z - distance, self.z - distance >= 0)]
        if distance > 0:
            events.append((1, self.z + distance, self.z + distance < ZL))
        return events

    def along_z(self, distance):
        for way, z, exists in self.events(distance):
            mine = self.slot(z, 0)
            src = mine
            if distance == 0:
                src = lambda: self.block
            else:
                self.net.arrive(way * 8 + distance, mine, self.down if way == 0 else self.up, exists)
            if distance < ZL - 1:
                if way == 0:
                    self.net.send(
                        distance + 1, src, mine, self.up, jnp.logical_and(exists, self.has_up)
                    )
                if way == 1 or distance == 0:
                    self.net.send(
                        8 + distance + 1, src, mine, self.down, jnp.logical_and(exists, self.has_down)
                    )
            cond = None if distance == 0 else exists
            self.net.send(16 + way * 8 + distance, src, mine, self.after, cond)
            self.net.send(32 + way * 8 + distance, src, mine, self.before, cond)
            self.share(way * 8 + distance, src, z, 0, cond)

    def along_y(self, distance):
        for way, z, exists in self.events(distance):
            cond = None if distance == 0 else exists
            index = way * 8 + distance
            self.net.arrive(16 + index, self.slot(z, -1), self.before, cond)
            if distance % 2 == 0:
                self.net.send(48 + index, self.slot(z, -1), self.slot(z, -1), self.after, cond)
            self.share(16 + index, self.slot(z, -1), z, -1, cond)
            self.net.arrive(32 + index, self.slot(z, 1), self.after, cond)
            if distance % 2 == 1:
                self.net.send(48 + index, self.slot(z, 1), self.slot(z, 1), self.before, cond)
            self.share(32 + index, self.slot(z, 1), z, 1, cond)

    def last(self):
        for distance in range(ZL):
            for way, z, exists in self.events(distance):
                cond = None if distance == 0 else exists
                source = self.before if distance % 2 == 0 else self.after
                self.net.arrive(48 + way * 8 + distance, self.slot(z, 2), source, cond)
                self.share(48 + way * 8 + distance, self.slot(z, 2), z, 2, cond)
        if self.other is not None:
            for distance in range(ZL):
                for way, z, exists in self.events(distance):
                    cond = None if distance == 0 else exists
                    for group, shift in enumerate((0, -1, 1, 2)):
                        where = z * YN + lax.rem(self.y + shift + YN, YN)
                        self.net.arrive(
                            64 + group * 16 + way * 8 + distance,
                            lambda where=where: self.other(where),
                            self.sibling,
                            cond,
                        )
        self.net.finish()


class ColGather:
    def __init__(self, block, out, send_sem, recv_sem):
        row, col = lax.axis_index("row"), lax.axis_index("col")
        self.high, self.x, self.core = col // (2 * XN), lax.rem(col // 2, XN), lax.rem(col, 2)
        self.block, self.out = block, out
        self.mate = (row, self.at(1, 0, 0))
        self.after = (row, self.at(0, 1, 0))
        self.before = (row, self.at(0, -1, 0))
        self.sibling = (row, self.at(0, 0, 1))
        self.net = Sender(send_sem, recv_sem)

    def partners(self):
        return [(self.mate, None), (self.after, None), (self.before, None), (self.sibling, None)]

    def at(self, high, shift, core):
        return (
            lax.rem(self.high + high, 2) * (2 * XN)
            + lax.rem(self.x + shift + XN, XN) * 2
            + lax.rem(self.core + core, 2)
        )

    def slot(self, high, shift, core=0):
        return lambda: self.out.at[self.at(high, shift, core)]

    def own(self, high):
        slot = self.slot(high, 0)
        src = slot
        if high == 0:
            src = lambda: self.block
            self.net.send(0, src, slot, self.mate)
        else:
            self.net.arrive(0, slot, self.mate)
        self.net.send(1 + high, src, slot, self.after)
        self.net.send(3 + high, src, slot, self.before)
        self.net.send(8 + high * 4, src, slot, self.sibling)

    def ring(self, high):
        self.net.arrive(1 + high, self.slot(high, -1), self.before)
        if high == 0:
            self.net.send(5, self.slot(high, -1), self.slot(high, -1), self.after)
        self.net.send(8 + high * 4 + 3, self.slot(high, -1), self.slot(high, -1), self.sibling)
        self.net.arrive(3 + high, self.slot(high, 1), self.after)
        if high == 1:
            self.net.send(6, self.slot(high, 1), self.slot(high, 1), self.before)
        self.net.send(8 + high * 4 + 1, self.slot(high, 1), self.slot(high, 1), self.sibling)

    def far(self, high):
        self.net.arrive(5 + high, self.slot(high, 2), self.before if high == 0 else self.after)
        self.net.send(8 + high * 4 + 2, self.slot(high, 2), self.slot(high, 2), self.sibling)

    def last(self):
        for high in range(2):
            for shift in range(XN):
                self.net.arrive(8 + high * 4 + shift, self.slot(high, shift, 1), self.sibling)
        self.net.finish()


def project(all_weight, hidden, query_ref, kv_ref, query_sum, kv_sum):
    query_sum[...] = jnp.zeros_like(query_sum)
    kv_sum[...] = jnp.zeros_like(kv_sum)

    @pl.loop(0, 4 * XN)
    def _(block):
        def columns(first):
            return jnp.concatenate(
                [
                    all_weight[2 * block, pl.ds(first, PIECE), :],
                    all_weight[2 * block + 1, pl.ds(first, PIECE), :],
                ],
                axis=0,
            )

        def narrow(piece):
            packed = all_weight[piece, pl.ds(KV_AT, PIECE // 2), :].astype(jnp.float32)
            return jnp.concatenate([packed[:, :HD], packed[:, HD:]], axis=0)

        mine = hidden[block]
        for half in range(2):
            query_sum[:, pl.ds(half * 128, 128)] += jnp.dot(
                mine, columns(Q_AT + half * PIECE), preferred_element_type=jnp.float32
            )
        used = jnp.concatenate([narrow(2 * block), narrow(2 * block + 1)], axis=0)
        kv_sum[...] += jnp.dot(
            mine, used.astype(jnp.bfloat16), preferred_element_type=jnp.float32
        )

    query_ref[...] = query_sum[...].astype(jnp.bfloat16)
    kv_ref[...] = jnp.concatenate([kv_sum[:HALF], kv_sum[HALF:]], axis=1).astype(jnp.bfloat16)


def normalise(all_token, gain_ref, hidden, squares):
    squares[...] = jnp.zeros_like(squares)

    @pl.loop(0, 4 * XN)
    def _(block):
        wide = all_token[block].astype(jnp.float32)
        squares[...] += wide * wide

    tail = squares[TOK:]
    tail = jnp.concatenate(
        [
            jnp.sum(tail[:, :64], axis=1, keepdims=True),
            jnp.sum(tail[:, 64:], axis=1, keepdims=True),
        ],
        axis=0,
    )
    mean = (jnp.sum(squares[:TOK], axis=1, keepdims=True) + tail) * (1.0 / WIDTH)
    inverse = lax.rsqrt(mean + 1e-05)

    @pl.loop(0, 4 * XN)
    def _(block):
        rows = unfold(all_token[block].astype(jnp.float32))
        hidden[block] = (rows * inverse * gain_ref[block]).astype(jnp.bfloat16)


def gather_kernel(
    weight_ref, token_ref, gain_ref, all_weight, query_ref, kv_ref, all_token, hidden, squares,
    query_sum, kv_sum, rs, rr, cs, cr, local_sem,
):
    rows = RowGather(weight_ref, lambda index: all_weight.at[index], rs, rr)
    cols = ColGather(token_ref, all_token, cs, cr)
    greet(rows.partners() + cols.partners())
    cols.own(0)
    rows.along_z(0)
    own_weight = pltpu.make_async_copy(weight_ref, all_weight.at[rows.row], local_sem.at[0])
    own_token = pltpu.make_async_copy(
        token_ref, all_token.at[lax.axis_index("col")], local_sem.at[1]
    )
    own_weight.start()
    own_token.start()
    rows.along_z(1)
    rows.along_y(0)
    cols.ring(0)
    rows.along_z(2)
    rows.along_y(1)
    cols.own(1)
    rows.along_z(3)
    rows.along_y(2)
    cols.far(0)
    rows.along_z(4)
    rows.along_y(3)
    cols.ring(1)
    rows.along_z(5)
    rows.along_y(4)
    cols.far(1)
    rows.along_z(6)
    rows.along_y(5)
    rows.along_z(7)
    rows.along_y(6)
    cols.last()
    own_token.wait()
    normalise(all_token, gain_ref, hidden, squares)
    rows.along_y(7)
    rows.last()
    own_weight.wait()
    project(all_weight, hidden, query_ref, kv_ref, query_sum, kv_sum)


def vmem():
    return pl.BlockSpec(memory_space=pltpu.VMEM)


def gather_first(weight_block, token_block, gain):
    return pl.pallas_call(
        gather_kernel,
        out_shape=(
            jax.ShapeDtypeStruct((ZL * YN,) + weight_block.shape, jnp.bfloat16),
            jax.ShapeDtypeStruct((TOK, 256), jnp.bfloat16),
            jax.ShapeDtypeStruct((HALF, 128), jnp.bfloat16),
        ),
        in_specs=[vmem()] * 3,
        out_specs=(vmem(),) * 3,
        scratch_shapes=[
            pltpu.VMEM((4 * XN, FOLD, 128), jnp.bfloat16),
            pltpu.VMEM((4 * XN, TOK, FEAT), jnp.bfloat16),
            pltpu.VMEM((FOLD, 128), jnp.float32),
            pltpu.VMEM((TOK, 256), jnp.float32),
            pltpu.VMEM((TOK, HD), jnp.float32),
            pltpu.SemaphoreType.DMA((ROW_COPIES,)),
            pltpu.SemaphoreType.DMA((ROW_COPIES,)),
            pltpu.SemaphoreType.DMA((COL_COPIES,)),
            pltpu.SemaphoreType.DMA((COL_COPIES,)),
            pltpu.SemaphoreType.DMA((2,)),
        ],
        compiler_params=pltpu.CompilerParams(
            collective_id=0, has_side_effects=True, vmem_limit_bytes=40 * 1024 * 1024
        ),
    )(weight_block, token_block, gain)


def kv_kernel(block_ref, out_ref, send_sem, recv_sem, local_sem):
    core = lax.rem(lax.axis_index("col"), 2)
    rows = RowGather(
        block_ref,
        lambda index: out_ref.at[core, index],
        send_sem,
        recv_sem,
        lambda index: out_ref.at[1 - core, index],
    )
    greet(rows.partners() + [(rows.sibling, None)])
    rows.along_z(0)
    own = pltpu.make_async_copy(block_ref, out_ref.at[core, rows.row], local_sem.at[0])
    own.start()
    for distance in range(1, ZL):
        rows.along_z(distance)
        rows.along_y(distance - 1)
    rows.along_y(ZL - 1)
    rows.last()
    own.wait()


def gather_kv(block):
    return pl.pallas_call(
        kv_kernel,
        out_shape=jax.ShapeDtypeStruct((2, ZL * YN) + block.shape, jnp.bfloat16),
        in_specs=[vmem()],
        out_specs=vmem(),
        scratch_shapes=[
            pltpu.SemaphoreType.DMA((SHARED_COPIES,)),
            pltpu.SemaphoreType.DMA((SHARED_COPIES,)),
            pltpu.SemaphoreType.DMA((1,)),
        ],
        compiler_params=pltpu.CompilerParams(
            collective_id=1, has_side_effects=True, vmem_limit_bytes=40 * 1024 * 1024
        ),
    )(block)


ORDER = ((1, 2), (0, 2), (1, 1), (1, 3), (0, 3), (0, 1), (1, 0), (0, 0))


def out_kernel(
    att_ref, weight_ref, token_ref, out_ref, first, landed, second, ring, keep, mate_out, mate_in,
    send_sem, recv_sem,
):
    row, col = lax.axis_index("row"), lax.axis_index("col")
    high, x, core = col // (2 * XN), lax.rem(col // 2, XN), lax.rem(col, 2)

    def at(dh, dx, dc):
        return (
            lax.rem(high + dh, 2) * (2 * XN) + lax.rem(x + dx + XN, XN) * 2 + lax.rem(core + dc, 2)
        )

    mate, after, before, sibling = (
        (row, at(1, 0, 0)), (row, at(0, 1, 0)), (row, at(0, -1, 0)), (row, at(0, 0, 1)),
    )
    greet([(mate, None), (after, None), (before, None), (sibling, None)])
    net = Sender(send_sem, recv_sem)

    def share(block):
        product = jnp.zeros((TOK, FEAT), jnp.float32)
        for half in range(2):
            columns = jnp.concatenate(
                [
                    weight_ref[2 * block + piece, pl.ds(O_AT + half * PIECE, PIECE), :]
                    for piece in range(2)
                ],
                axis=0,
            )
            product += lax.dot_general(
                att_ref[:, pl.ds(half * 128, 128)],
                columns,
                (((1,), (1,)), ((), ())),
                preferred_element_type=jnp.float32,
            )
        return fold(product)

    for k, (dh, dx) in enumerate(ORDER):
        first[k] = share(at(dh, dx, 1)).astype(jnp.bfloat16)
        net.send(k, lambda k=k: first.at[k], lambda k=k: landed.at[k], sibling)

    def summed(k):
        dh, dx = ORDER[k]
        own = share(at(dh, dx, 0))
        net.arrive(k, lambda: landed.at[k], sibling)
        return own + landed[k].astype(jnp.float32)

    def pass_on(index, value, device):
        second[index] = value.astype(jnp.bfloat16)
        net.send(8 + index, lambda: second.at[index], lambda: ring.at[index], device)

    def arrived(index, device):
        net.arrive(8 + index, lambda: ring.at[index], device)
        return ring[index].astype(jnp.float32)

    pass_on(0, summed(0), before)
    pass_on(1, summed(1), after)
    pass_on(2, summed(2), after)
    keep[0] = summed(3)
    pass_on(4, keep[0] + arrived(0, after), before)
    pass_on(3, summed(4), before)
    keep[1] = summed(5)
    pass_on(5, keep[1] + arrived(1, before), after)
    keep[2] = summed(6)
    mate_out[...] = (keep[2] + arrived(2, before) + arrived(4, after)).astype(jnp.bfloat16)
    net.send(14, lambda: mate_out, lambda: mate_in, mate)
    keep[3] = summed(7) + token_ref[...].astype(jnp.float32)
    total = keep[3] + arrived(3, after) + arrived(5, before)
    net.arrive(14, lambda: mate_in, mate)
    out_ref[...] = (total + mate_in[...].astype(jnp.float32)).astype(jnp.bfloat16)
    net.finish()


def project_out(att, weights, tokens):
    block = (FOLD, 128)
    return pl.pallas_call(
        out_kernel,
        out_shape=jax.ShapeDtypeStruct(block, jnp.bfloat16),
        in_specs=[vmem()] * 3,
        out_specs=vmem(),
        scratch_shapes=[
            pltpu.VMEM((8,) + block, jnp.bfloat16),
            pltpu.VMEM((8,) + block, jnp.bfloat16),
            pltpu.VMEM((6,) + block, jnp.bfloat16),
            pltpu.VMEM((6,) + block, jnp.bfloat16),
            pltpu.VMEM((4,) + block, jnp.float32),
            pltpu.VMEM(block, jnp.bfloat16),
            pltpu.VMEM(block, jnp.bfloat16),
            pltpu.SemaphoreType.DMA((16,)),
            pltpu.SemaphoreType.DMA((16,)),
        ],
        compiler_params=pltpu.CompilerParams(
            collective_id=2, has_side_effects=True, vmem_limit_bytes=40 * 1024 * 1024
        ),
    )(att, weights, tokens)


def body(
    prefill_hidden,
    decode_hidden,
    norm_gain,
    query_weight,
    kv_weight,
    out_weight,
    sink_logits,
    key_pool,
    value_pool,
    lengths,
    page_table,
):
    spans, span_rows, col_width = prefill_hidden.shape
    decode_rows = decode_hidden.shape[0]
    heads = query_weight.shape[1] // HD
    col_index = lax.axis_index("col")
    row_index = lax.axis_index("row")
    core = col_index % 2
    kv_head = col_index * heads // (HQ // KV)
    half_rows = (spans // 2) * span_rows
    gap = HALF - half_rows - decode_rows

    def padded(array, axis):
        pads = [(0, 0)] * array.ndim
        pads[axis] = (0, PIECE - array.shape[axis])
        return jnp.pad(array, pads)

    def two_halves(prefill, decode):
        wide = prefill.shape[1]
        return jnp.concatenate(
            [
                prefill[:half_rows],
                decode,
                jnp.zeros((gap, wide), decode.dtype),
                prefill[half_rows:],
                jnp.zeros((HALF - half_rows, wide), decode.dtype),
            ],
            axis=0,
        )

    kv_mine = padded(
        lax.dynamic_slice(
            kv_weight, (0, core, kv_head * HD), (kv_weight.shape[0], 1, HD)
        ).reshape(-1, HD),
        0,
    )
    query_mine = padded(query_weight, 0)
    out_mine = padded(out_weight.T, 0)
    weight_block = jnp.concatenate(
        [
            query_mine[:, :128],
            query_mine[:, 128:],
            out_mine[:, :128],
            out_mine[:, 128:],
            jnp.concatenate([kv_mine[: PIECE // 2], kv_mine[PIECE // 2 :]], axis=1),
        ],
        axis=0,
    )
    part = col_width // 2
    token_rows = two_halves(prefill_hidden.reshape(-1, col_width), decode_hidden)
    token_block = fold(
        jnp.concatenate(
            [padded(token_rows[:, :part], 1), padded(token_rows[:, part:], 1)], axis=1
        )
    )
    gain = (
        padded(norm_gain.astype(jnp.float32).reshape(-1, part), 1).reshape(4 * XN, 1, FEAT)
    )
    all_weight, queries, kv_block = gather_first(weight_block, token_block, gain)
    kv_all = gather_kv(kv_block)
    score_scale = 1.0 / math.sqrt(HD)
    sink = sink_logits.astype(jnp.float32)
    query_pre = jnp.concatenate(
        [queries[:half_rows], queries[HALF : HALF + half_rows]], axis=0
    ).reshape(spans, span_rows, heads, HD)
    key_pair, value_pair = [
        jnp.concatenate(
            [
                kv_all[which, :, :half_rows, side * HD : (side + 1) * HD]
                .reshape(-1, spans // 2, span_rows, HD)
                .transpose(1, 0, 2, 3)
                .reshape(spans // 2, -1, HD)
                for side in range(2)
            ],
            axis=0,
        )
        for which in range(2)
    ]
    positions = row_index * span_rows + jnp.arange(span_rows, dtype=jnp.int32)
    scores = (
        jnp.einsum("sqgd,spd->sgqp", query_pre, key_pair, preferred_element_type=jnp.float32)
        * score_scale
    )
    key_pos = jnp.arange(key_pair.shape[1], dtype=jnp.int32)
    scores = jnp.where(key_pos[None, :] <= positions[:, None], scores, -jnp.inf)
    sink_pre = sink[None, :, None]
    highest = jnp.maximum(jnp.max(scores, axis=-1), sink_pre)
    probs = jnp.exp(scores - highest[..., None])
    denominator = jnp.sum(probs, axis=-1) + jnp.exp(sink_pre - highest)
    weighted = jnp.einsum(
        "sgqp,spd->sgqd",
        probs.astype(jnp.bfloat16),
        value_pair,
        preferred_element_type=jnp.float32,
    )
    prefill_att = (
        (weighted / denominator[..., None])
        .transpose(0, 2, 1, 3)
        .reshape(spans * span_rows, heads * HD)
        .astype(jnp.bfloat16)
    )
    query_dec = queries[half_rows : half_rows + decode_rows].reshape(decode_rows, heads, HD)
    new_rows = lax.dynamic_index_in_dim(kv_all, row_index, 1, keepdims=False)
    key_new = new_rows[0, half_rows : half_rows + decode_rows, :HD]
    value_new = new_rows[1, half_rows : half_rows + decode_rows, :HD]
    table = page_table.reshape(decode_rows, -1)
    page_len = key_pool.shape[1]
    key_mine = lax.dynamic_slice_in_dim(key_pool, kv_head * HD, HD, 2)
    value_mine = lax.dynamic_slice_in_dim(value_pool, kv_head * HD, HD, 2)
    cached = table.shape[1] * page_len
    key_cache = key_mine[table].reshape(decode_rows, cached, HD)
    value_cache = value_mine[table].reshape(decode_rows, cached, HD)
    cache_scores = (
        jnp.einsum("sgd,std->sgt", query_dec, key_cache, preferred_element_type=jnp.float32)
        * score_scale
    )
    live = jnp.arange(cached, dtype=jnp.int32)[None, :] < lengths.reshape(decode_rows)[:, None]
    cache_scores = jnp.where(live[:, None, :], cache_scores, -jnp.inf)
    self_scores = (
        jnp.einsum("sgd,sd->sg", query_dec, key_new, preferred_element_type=jnp.float32)
        * score_scale
    )
    highest = jnp.maximum(jnp.maximum(jnp.max(cache_scores, axis=-1), self_scores), sink[None])
    cache_probs = jnp.exp(cache_scores - highest[..., None])
    self_probs = jnp.exp(self_scores - highest)
    denom_dec = jnp.sum(cache_probs, axis=-1) + self_probs + jnp.exp(sink[None] - highest)
    decode_sum = jnp.einsum(
        "sgt,std->sgd",
        cache_probs.astype(jnp.bfloat16),
        value_cache,
        preferred_element_type=jnp.float32,
    )
    decode_sum = (
        decode_sum
        + self_probs.astype(jnp.bfloat16).astype(jnp.float32)[..., None]
        * value_new.astype(jnp.float32)[:, None, :]
    )
    decode_att = (
        (decode_sum / denom_dec[..., None]).reshape(decode_rows, heads * HD).astype(jnp.bfloat16)
    )
    result = unfold(project_out(two_halves(prefill_att, decode_att), all_weight, token_block))
    result = jnp.concatenate([result[:, :part], result[:, PIECE : PIECE + part]], axis=1)
    prefill_out = jnp.concatenate([result[:half_rows], result[HALF : HALF + half_rows]], axis=0)
    return (
        prefill_out.reshape(spans, span_rows, col_width),
        result[half_rows : half_rows + decode_rows],
    )


def solution(mesh):
    in_specs = (
        P(None, "row", "col"),
        P("row", "col"),
        P(),
        P("row", "col"),
        P("row", None, None),
        P("col", "row"),
        P("col"),
        P("row", None, None),
        P("row", None, None),
        P("row", None),
        P("row", None),
    )
    out_specs = (P(None, "row", "col"), P("row", "col"))
    return jax.shard_map(body, mesh=mesh, in_specs=in_specs, out_specs=out_specs, check_vma=False)
```

```python
import math

import jax
import jax.numpy as jnp
from jax import lax
from jax.experimental import pallas as pl
from jax.experimental.pallas import tpu as pltpu
from jax.sharding import PartitionSpec as P

HQ = 64
KV = 8
HD = 64
WIDTH = 2880
ZL = 8
YN = 4
XN = 4
TOK = 272
HALF = TOK // 2
FOLD = TOK + HALF
FEAT = 192
MESH = pl.DeviceIdType.MESH
ROW_COPIES = 64
PIECE = FEAT // 2
Q_AT, O_AT, KV_AT = 0, 2 * PIECE, 4 * PIECE
COL_COPIES = 24


def fold(rows):
    tail = jnp.concatenate([rows[:HALF, 128:FEAT], rows[HALF:, 128:FEAT]], axis=1)
    return jnp.concatenate([rows[:, :128], tail], axis=0)


def unfold(folded):
    head, tail = folded[..., :TOK, :], folded[..., TOK:, :]
    tail = jnp.concatenate([tail[..., :64], tail[..., 64:]], axis=-2)
    return jnp.concatenate([head, tail], axis=-1)


class Sender:
    def __init__(self, send_sem, recv_sem):
        self.send_sem, self.recv_sem = send_sem, recv_sem
        self.started = []

    def copy(self, index, src, dst, device):
        return pltpu.make_async_remote_copy(
            src_ref=src(),
            dst_ref=dst(),
            send_sem=self.send_sem.at[index],
            recv_sem=self.recv_sem.at[index],
            device_id=device,
            device_id_type=MESH,
        )

    def run(self, cond, action):
        if cond is None:
            action()
        else:
            pl.when(cond)(action)

    def send(self, index, src, dst, device, cond=None):
        self.run(cond, lambda: self.copy(index, src, dst, device).start())
        self.started.append((index, src, dst, device, cond))

    def arrive(self, index, slot, device, cond=None):
        self.run(cond, lambda: self.copy(index, slot, slot, device).wait_recv())

    def finish(self):
        for index, src, dst, device, cond in self.started:
            self.run(cond, lambda: self.copy(index, src, dst, device).wait_send())


def greet(pairs):
    barrier = pltpu.get_barrier_semaphore()
    for device, cond in pairs:
        def hello(device=device):
            pl.semaphore_signal(barrier, inc=1, device_id=device, device_id_type=MESH)

        if cond is None:
            hello()
        else:
            pl.when(cond)(hello)
    peers = sum(1 if cond is None else cond.astype(jnp.int32) for _, cond in pairs)
    pl.semaphore_wait(barrier, peers)


class RowGather:
    def __init__(self, block, out, send_sem, recv_sem):
        row, col = lax.axis_index("row"), lax.axis_index("col")
        self.row = row
        self.z, self.y = row // YN, lax.rem(row, YN)
        self.block, self.out = block, out
        self.up = (row + YN, col)
        self.down = (row - YN, col)
        self.has_up = self.z < ZL - 1
        self.has_down = self.z > 0
        self.after = (self.z * YN + lax.rem(self.y + 1, YN), col)
        self.before = (self.z * YN + lax.rem(self.y + YN - 1, YN), col)
        self.net = Sender(send_sem, recv_sem)

    def partners(self):
        return [
            (self.up, self.has_up),
            (self.down, self.has_down),
            (self.after, None),
            (self.before, None),
        ]

    def slot(self, z, shift):
        return lambda: self.out(z * YN + lax.rem(self.y + shift + YN, YN))

    def events(self, distance):
        events = [(0, self.z - distance, self.z - distance >= 0)]
        if distance > 0:
            events.append((1, self.z + distance, self.z + distance < ZL))
        return events

    def along_z(self, distance):
        for way, z, exists in self.events(distance):
            mine = self.slot(z, 0)
            src = mine
            if distance == 0:
                src = lambda: self.block
            else:
                self.net.arrive(way * 8 + distance, mine, self.down if way == 0 else self.up, exists)
            if distance < ZL - 1:
                if way == 0:
                    self.net.send(
                        distance + 1, src, mine, self.up, jnp.logical_and(exists, self.has_up)
                    )
                if way == 1 or distance == 0:
                    self.net.send(
                        8 + distance + 1, src, mine, self.down, jnp.logical_and(exists, self.has_down)
                    )
            cond = None if distance == 0 else exists
            self.net.send(16 + way * 8 + distance, src, mine, self.after, cond)
            self.net.send(32 + way * 8 + distance, src, mine, self.before, cond)

    def along_y(self, distance):
        for way, z, exists in self.events(distance):
            cond = None if distance == 0 else exists
            index = way * 8 + distance
            self.net.arrive(16 + index, self.slot(z, -1), self.before, cond)
            if distance % 2 == 0:
                self.net.send(48 + index, self.slot(z, -1), self.slot(z, -1), self.after, cond)
            self.net.arrive(32 + index, self.slot(z, 1), self.after, cond)
            if distance % 2 == 1:
                self.net.send(48 + index, self.slot(z, 1), self.slot(z, 1), self.before, cond)

    def last(self):
        for distance in range(ZL):
            for way, z, exists in self.events(distance):
                cond = None if distance == 0 else exists
                source = self.before if distance % 2 == 0 else self.after
                self.net.arrive(48 + way * 8 + distance, self.slot(z, 2), source, cond)
        self.net.finish()


class ColGather:
    def __init__(self, block, out, send_sem, recv_sem):
        row, col = lax.axis_index("row"), lax.axis_index("col")
        self.high, self.x, self.core = col // (2 * XN), lax.rem(col // 2, XN), lax.rem(col, 2)
        self.block, self.out = block, out
        self.mate = (row, self.at(1, 0, 0))
        self.after = (row, self.at(0, 1, 0))
        self.before = (row, self.at(0, -1, 0))
        self.sibling = (row, self.at(0, 0, 1))
        self.net = Sender(send_sem, recv_sem)

    def partners(self):
        return [(self.mate, None), (self.after, None), (self.before, None), (self.sibling, None)]

    def at(self, high, shift, core):
        return (
            lax.rem(self.high + high, 2) * (2 * XN)
            + lax.rem(self.x + shift + XN, XN) * 2
            + lax.rem(self.core + core, 2)
        )

    def slot(self, high, shift, core=0):
        return lambda: self.out.at[self.at(high, shift, core)]

    def own(self, high):
        slot = self.slot(high, 0)
        src = slot
        if high == 0:
            src = lambda: self.block
            self.net.send(0, src, slot, self.mate)
        else:
            self.net.arrive(0, slot, self.mate)
        self.net.send(1 + high, src, slot, self.after)
        self.net.send(3 + high, src, slot, self.before)
        self.net.send(8 + high * 4, src, slot, self.sibling)

    def ring(self, high):
        self.net.arrive(1 + high, self.slot(high, -1), self.before)
        if high == 0:
            self.net.send(5, self.slot(high, -1), self.slot(high, -1), self.after)
        self.net.send(8 + high * 4 + 3, self.slot(high, -1), self.slot(high, -1), self.sibling)
        self.net.arrive(3 + high, self.slot(high, 1), self.after)
        if high == 1:
            self.net.send(6, self.slot(high, 1), self.slot(high, 1), self.before)
        self.net.send(8 + high * 4 + 1, self.slot(high, 1), self.slot(high, 1), self.sibling)

    def far(self, high):
        self.net.arrive(5 + high, self.slot(high, 2), self.before if high == 0 else self.after)
        self.net.send(8 + high * 4 + 2, self.slot(high, 2), self.slot(high, 2), self.sibling)

    def last(self):
        for high in range(2):
            for shift in range(XN):
                self.net.arrive(8 + high * 4 + shift, self.slot(high, shift, 1), self.sibling)
        self.net.finish()


def project(all_weight, hidden, query_ref, kv_ref, query_sum, kv_sum):
    query_sum[...] = jnp.zeros_like(query_sum)
    kv_sum[...] = jnp.zeros_like(kv_sum)

    @pl.loop(0, 4 * XN)
    def _(block):
        def columns(first):
            return jnp.concatenate(
                [
                    all_weight[2 * block, pl.ds(first, PIECE), :],
                    all_weight[2 * block + 1, pl.ds(first, PIECE), :],
                ],
                axis=0,
            )

        mine = hidden[block]
        for half in range(2):
            query_sum[:, pl.ds(half * 128, 128)] += jnp.dot(
                mine, columns(Q_AT + half * PIECE), preferred_element_type=jnp.float32
            )
        kv_sum[...] += jnp.dot(mine, columns(KV_AT), preferred_element_type=jnp.float32)

    query_ref[...] = query_sum[...].astype(jnp.bfloat16)
    kv_ref[...] = kv_sum[...].astype(jnp.bfloat16)


def normalise(all_token, gain_ref, hidden, squares):
    squares[...] = jnp.zeros_like(squares)

    @pl.loop(0, 4 * XN)
    def _(block):
        wide = all_token[block].astype(jnp.float32)
        squares[...] += wide * wide

    tail = squares[TOK:]
    tail = jnp.concatenate(
        [
            jnp.sum(tail[:, :64], axis=1, keepdims=True),
            jnp.sum(tail[:, 64:], axis=1, keepdims=True),
        ],
        axis=0,
    )
    mean = (jnp.sum(squares[:TOK], axis=1, keepdims=True) + tail) * (1.0 / WIDTH)
    inverse = lax.rsqrt(mean + 1e-05)

    @pl.loop(0, 4 * XN)
    def _(block):
        rows = unfold(all_token[block].astype(jnp.float32))
        hidden[block] = (rows * inverse * gain_ref[block]).astype(jnp.bfloat16)


def gather_kernel(
    weight_ref, token_ref, gain_ref, all_weight, query_ref, kv_ref, all_token, hidden, squares,
    query_sum, kv_sum, rs, rr, cs, cr, local_sem,
):
    rows = RowGather(weight_ref, lambda index: all_weight.at[index], rs, rr)
    cols = ColGather(token_ref, all_token, cs, cr)
    greet(rows.partners() + cols.partners())
    cols.own(0)
    rows.along_z(0)
    own_weight = pltpu.make_async_copy(weight_ref, all_weight.at[rows.row], local_sem.at[0])
    own_token = pltpu.make_async_copy(
        token_ref, all_token.at[lax.axis_index("col")], local_sem.at[1]
    )
    own_weight.start()
    own_token.start()
    rows.along_z(1)
    rows.along_y(0)
    cols.ring(0)
    rows.along_z(2)
    rows.along_y(1)
    cols.own(1)
    rows.along_z(3)
    rows.along_y(2)
    cols.far(0)
    rows.along_z(4)
    rows.along_y(3)
    cols.ring(1)
    rows.along_z(5)
    rows.along_y(4)
    cols.far(1)
    rows.along_z(6)
    rows.along_y(5)
    rows.along_z(7)
    rows.along_y(6)
    cols.last()
    own_token.wait()
    normalise(all_token, gain_ref, hidden, squares)
    rows.along_y(7)
    rows.last()
    own_weight.wait()
    project(all_weight, hidden, query_ref, kv_ref, query_sum, kv_sum)


def vmem():
    return pl.BlockSpec(memory_space=pltpu.VMEM)


def gather_first(weight_block, token_block, gain):
    return pl.pallas_call(
        gather_kernel,
        out_shape=(
            jax.ShapeDtypeStruct((ZL * YN,) + weight_block.shape, jnp.bfloat16),
            jax.ShapeDtypeStruct((TOK, 256), jnp.bfloat16),
            jax.ShapeDtypeStruct((TOK, 128), jnp.bfloat16),
        ),
        in_specs=[vmem()] * 3,
        out_specs=(vmem(),) * 3,
        scratch_shapes=[
            pltpu.VMEM((4 * XN, FOLD, 128), jnp.bfloat16),
            pltpu.VMEM((4 * XN, TOK, FEAT), jnp.bfloat16),
            pltpu.VMEM((FOLD, 128), jnp.float32),
            pltpu.VMEM((TOK, 256), jnp.float32),
            pltpu.VMEM((TOK, 128), jnp.float32),
            pltpu.SemaphoreType.DMA((ROW_COPIES,)),
            pltpu.SemaphoreType.DMA((ROW_COPIES,)),
            pltpu.SemaphoreType.DMA((COL_COPIES,)),
            pltpu.SemaphoreType.DMA((COL_COPIES,)),
            pltpu.SemaphoreType.DMA((2,)),
        ],
        compiler_params=pltpu.CompilerParams(
            collective_id=0, has_side_effects=True, vmem_limit_bytes=40 * 1024 * 1024
        ),
    )(weight_block, token_block, gain)


def kv_kernel(block_ref, out_ref, send_sem, recv_sem, local_sem):
    rows = RowGather(block_ref, lambda index: out_ref.at[index], send_sem, recv_sem)
    greet(rows.partners())
    rows.along_z(0)
    own = pltpu.make_async_copy(block_ref, out_ref.at[rows.row], local_sem.at[0])
    own.start()
    for distance in range(1, ZL):
        rows.along_z(distance)
        rows.along_y(distance - 1)
    rows.along_y(ZL - 1)
    rows.last()
    own.wait()


def gather_kv(block):
    return pl.pallas_call(
        kv_kernel,
        out_shape=jax.ShapeDtypeStruct((ZL * YN,) + block.shape, jnp.bfloat16),
        in_specs=[vmem()],
        out_specs=vmem(),
        scratch_shapes=[
            pltpu.SemaphoreType.DMA((ROW_COPIES,)),
            pltpu.SemaphoreType.DMA((ROW_COPIES,)),
            pltpu.SemaphoreType.DMA((1,)),
        ],
        compiler_params=pltpu.CompilerParams(
            collective_id=1, has_side_effects=True, vmem_limit_bytes=40 * 1024 * 1024
        ),
    )(block)


ORDER = ((1, 2), (0, 2), (1, 1), (1, 3), (0, 3), (0, 1), (1, 0), (0, 0))


def out_kernel(
    att_ref, weight_ref, token_ref, out_ref, first, landed, second, ring, keep, mate_out, mate_in,
    send_sem, recv_sem,
):
    row, col = lax.axis_index("row"), lax.axis_index("col")
    high, x, core = col // (2 * XN), lax.rem(col // 2, XN), lax.rem(col, 2)

    def at(dh, dx, dc):
        return (
            lax.rem(high + dh, 2) * (2 * XN) + lax.rem(x + dx + XN, XN) * 2 + lax.rem(core + dc, 2)
        )

    mate, after, before, sibling = (
        (row, at(1, 0, 0)), (row, at(0, 1, 0)), (row, at(0, -1, 0)), (row, at(0, 0, 1)),
    )
    greet([(mate, None), (after, None), (before, None), (sibling, None)])
    net = Sender(send_sem, recv_sem)

    def share(block):
        product = jnp.zeros((TOK, FEAT), jnp.float32)
        for half in range(2):
            columns = jnp.concatenate(
                [
                    weight_ref[2 * block + piece, pl.ds(O_AT + half * PIECE, PIECE), :]
                    for piece in range(2)
                ],
                axis=0,
            )
            product += lax.dot_general(
                att_ref[:, pl.ds(half * 128, 128)],
                columns,
                (((1,), (1,)), ((), ())),
                preferred_element_type=jnp.float32,
            )
        return fold(product)

    for k, (dh, dx) in enumerate(ORDER):
        first[k] = share(at(dh, dx, 1)).astype(jnp.bfloat16)
        net.send(k, lambda k=k: first.at[k], lambda k=k: landed.at[k], sibling)

    def summed(k):
        dh, dx = ORDER[k]
        own = share(at(dh, dx, 0))
        net.arrive(k, lambda: landed.at[k], sibling)
        return own + landed[k].astype(jnp.float32)

    def pass_on(index, value, device):
        second[index] = value.astype(jnp.bfloat16)
        net.send(8 + index, lambda: second.at[index], lambda: ring.at[index], device)

    def arrived(index, device):
        net.arrive(8 + index, lambda: ring.at[index], device)
        return ring[index].astype(jnp.float32)

    pass_on(0, summed(0), before)
    pass_on(1, summed(1), after)
    pass_on(2, summed(2), after)
    keep[0] = summed(3)
    pass_on(4, keep[0] + arrived(0, after), before)
    pass_on(3, summed(4), before)
    keep[1] = summed(5)
    pass_on(5, keep[1] + arrived(1, before), after)
    keep[2] = summed(6)
    mate_out[...] = (keep[2] + arrived(2, before) + arrived(4, after)).astype(jnp.bfloat16)
    net.send(14, lambda: mate_out, lambda: mate_in, mate)
    keep[3] = summed(7) + token_ref[...].astype(jnp.float32)
    total = keep[3] + arrived(3, after) + arrived(5, before)
    net.arrive(14, lambda: mate_in, mate)
    out_ref[...] = (total + mate_in[...].astype(jnp.float32)).astype(jnp.bfloat16)
    net.finish()


def project_out(att, weights, tokens):
    block = (FOLD, 128)
    return pl.pallas_call(
        out_kernel,
        out_shape=jax.ShapeDtypeStruct(block, jnp.bfloat16),
        in_specs=[vmem()] * 3,
        out_specs=vmem(),
        scratch_shapes=[
            pltpu.VMEM((8,) + block, jnp.bfloat16),
            pltpu.VMEM((8,) + block, jnp.bfloat16),
            pltpu.VMEM((6,) + block, jnp.bfloat16),
            pltpu.VMEM((6,) + block, jnp.bfloat16),
            pltpu.VMEM((4,) + block, jnp.float32),
            pltpu.VMEM(block, jnp.bfloat16),
            pltpu.VMEM(block, jnp.bfloat16),
            pltpu.SemaphoreType.DMA((16,)),
            pltpu.SemaphoreType.DMA((16,)),
        ],
        compiler_params=pltpu.CompilerParams(
            collective_id=2, has_side_effects=True, vmem_limit_bytes=40 * 1024 * 1024
        ),
    )(att, weights, tokens)


def body(
    prefill_hidden,
    decode_hidden,
    norm_gain,
    query_weight,
    kv_weight,
    out_weight,
    sink_logits,
    key_pool,
    value_pool,
    lengths,
    page_table,
):
    spans, span_rows, col_width = prefill_hidden.shape
    decode_rows = decode_hidden.shape[0]
    heads = query_weight.shape[1] // HD
    col_index = lax.axis_index("col")
    row_index = lax.axis_index("row")
    kv_head = col_index * heads // (HQ // KV)
    half_rows = (spans // 2) * span_rows
    gap = HALF - half_rows - decode_rows

    def padded(array, axis):
        pads = [(0, 0)] * array.ndim
        pads[axis] = (0, PIECE - array.shape[axis])
        return jnp.pad(array, pads)

    def two_halves(prefill, decode):
        wide = prefill.shape[1]
        return jnp.concatenate(
            [
                prefill[:half_rows],
                decode,
                jnp.zeros((gap, wide), decode.dtype),
                prefill[half_rows:],
                jnp.zeros((HALF - half_rows, wide), decode.dtype),
            ],
            axis=0,
        )

    kv_mine = padded(
        jnp.concatenate(
            [
                lax.dynamic_slice_in_dim(kv_weight[:, which], kv_head * HD, HD, 1)
                for which in range(2)
            ],
            axis=1,
        ),
        0,
    )
    query_mine = padded(query_weight, 0)
    out_mine = padded(out_weight.T, 0)
    weight_block = jnp.concatenate(
        [
            query_mine[:, :128],
            query_mine[:, 128:],
            out_mine[:, :128],
            out_mine[:, 128:],
            kv_mine,
        ],
        axis=0,
    )
    part = col_width // 2
    token_rows = two_halves(prefill_hidden.reshape(-1, col_width), decode_hidden)
    token_block = fold(
        jnp.concatenate(
            [padded(token_rows[:, :part], 1), padded(token_rows[:, part:], 1)], axis=1
        )
    )
    gain = (
        padded(norm_gain.astype(jnp.float32).reshape(-1, part), 1).reshape(4 * XN, 1, FEAT)
    )
    all_weight, queries, kv_rows = gather_first(weight_block, token_block, gain)
    kv_all = (
        gather_kv(jnp.concatenate([kv_rows[:half_rows], kv_rows[HALF : HALF + half_rows]], axis=0))
        .reshape(-1, spans, span_rows, 2 * HD)
        .transpose(1, 0, 2, 3)
        .reshape(spans, -1, 2 * HD)
    )
    score_scale = 1.0 / math.sqrt(HD)
    sink = sink_logits.astype(jnp.float32)
    query_pre = jnp.concatenate(
        [queries[:half_rows], queries[HALF : HALF + half_rows]], axis=0
    ).reshape(spans, span_rows, heads, HD)
    key_pair, value_pair = kv_all[..., :HD], kv_all[..., HD:]
    positions = row_index * span_rows + jnp.arange(span_rows, dtype=jnp.int32)
    scores = (
        jnp.einsum("sqgd,spd->sgqp", query_pre, key_pair, preferred_element_type=jnp.float32)
        * score_scale
    )
    key_pos = jnp.arange(key_pair.shape[1], dtype=jnp.int32)
    scores = jnp.where(key_pos[None, :] <= positions[:, None], scores, -jnp.inf)
    sink_pre = sink[None, :, None]
    highest = jnp.maximum(jnp.max(scores, axis=-1), sink_pre)
    probs = jnp.exp(scores - highest[..., None])
    denominator = jnp.sum(probs, axis=-1) + jnp.exp(sink_pre - highest)
    weighted = jnp.einsum(
        "sgqp,spd->sgqd",
        probs.astype(jnp.bfloat16),
        value_pair,
        preferred_element_type=jnp.float32,
    )
    prefill_att = (
        (weighted / denominator[..., None])
        .transpose(0, 2, 1, 3)
        .reshape(spans * span_rows, heads * HD)
        .astype(jnp.bfloat16)
    )
    query_dec = queries[half_rows : half_rows + decode_rows].reshape(decode_rows, heads, HD)
    new_rows = kv_rows[half_rows : half_rows + decode_rows]
    key_new, value_new = new_rows[:, :HD], new_rows[:, HD:]
    table = page_table.reshape(decode_rows, -1)
    page_len = key_pool.shape[1]
    key_mine = lax.dynamic_slice_in_dim(key_pool, kv_head * HD, HD, 2)
    value_mine = lax.dynamic_slice_in_dim(value_pool, kv_head * HD, HD, 2)
    cached = table.shape[1] * page_len
    key_cache = key_mine[table].reshape(decode_rows, cached, HD)
    value_cache = value_mine[table].reshape(decode_rows, cached, HD)
    cache_scores = (
        jnp.einsum("sgd,std->sgt", query_dec, key_cache, preferred_element_type=jnp.float32)
        * score_scale
    )
    live = jnp.arange(cached, dtype=jnp.int32)[None, :] < lengths.reshape(decode_rows)[:, None]
    cache_scores = jnp.where(live[:, None, :], cache_scores, -jnp.inf)
    self_scores = (
        jnp.einsum("sgd,sd->sg", query_dec, key_new, preferred_element_type=jnp.float32)
        * score_scale
    )
    highest = jnp.maximum(jnp.maximum(jnp.max(cache_scores, axis=-1), self_scores), sink[None])
    cache_probs = jnp.exp(cache_scores - highest[..., None])
    self_probs = jnp.exp(self_scores - highest)
    denom_dec = jnp.sum(cache_probs, axis=-1) + self_probs + jnp.exp(sink[None] - highest)
    decode_sum = jnp.einsum(
        "sgt,std->sgd",
        cache_probs.astype(jnp.bfloat16),
        value_cache,
        preferred_element_type=jnp.float32,
    )
    decode_sum = (
        decode_sum
        + self_probs.astype(jnp.bfloat16).astype(jnp.float32)[..., None]
        * value_new.astype(jnp.float32)[:, None, :]
    )
    decode_att = (
        (decode_sum / denom_dec[..., None]).reshape(decode_rows, heads * HD).astype(jnp.bfloat16)
    )
    result = unfold(project_out(two_halves(prefill_att, decode_att), all_weight, token_block))
    result = jnp.concatenate([result[:, :part], result[:, PIECE : PIECE + part]], axis=1)
    prefill_out = jnp.concatenate([result[:half_rows], result[HALF : HALF + half_rows]], axis=0)
    return (
        prefill_out.reshape(spans, span_rows, col_width),
        result[half_rows : half_rows + decode_rows],
    )


def solution(mesh):
    in_specs = (
        P(None, "row", "col"),
        P("row", "col"),
        P(),
        P("row", "col"),
        P("row", None, None),
        P("col", "row"),
        P("col"),
        P("row", None, None),
        P("row", None, None),
        P("row", None),
        P("row", None),
    )
    out_specs = (P(None, "row", "col"), P("row", "col"))
    return jax.shard_map(body, mesh=mesh, in_specs=in_specs, out_specs=out_specs, check_vma=False)
```

```python
import math

import jax
import jax.numpy as jnp
from jax import lax
from jax.experimental import pallas as pl
from jax.experimental.pallas import tpu as pltpu
from jax.sharding import PartitionSpec as P

HQ = 64
KV = 8
HD = 64
WIDTH = 2880
ZL = 8
YN = 4
XN = 4
TOK = 272
HALF = TOK // 2
FOLD = TOK + HALF
FEAT = 192
MESH = pl.DeviceIdType.MESH
ROW_COPIES = 64
PIECE = FEAT // 2
Q_AT, O_AT, KV_AT = 0, 2 * PIECE, 4 * PIECE
COL_COPIES = 24


def fold(rows):
    tail = jnp.concatenate([rows[:HALF, 128:FEAT], rows[HALF:, 128:FEAT]], axis=1)
    return jnp.concatenate([rows[:, :128], tail], axis=0)


def unfold(folded):
    head, tail = folded[..., :TOK, :], folded[..., TOK:, :]
    tail = jnp.concatenate([tail[..., :64], tail[..., 64:]], axis=-2)
    return jnp.concatenate([head, tail], axis=-1)


class Sender:
    def __init__(self, send_sem, recv_sem):
        self.send_sem, self.recv_sem = send_sem, recv_sem
        self.started = []

    def copy(self, index, src, dst, device):
        return pltpu.make_async_remote_copy(
            src_ref=src(),
            dst_ref=dst(),
            send_sem=self.send_sem.at[index],
            recv_sem=self.recv_sem.at[index],
            device_id=device,
            device_id_type=MESH,
        )

    def run(self, cond, action):
        if cond is None:
            action()
        else:
            pl.when(cond)(action)

    def send(self, index, src, dst, device, cond=None):
        self.run(cond, lambda: self.copy(index, src, dst, device).start())
        self.started.append((index, src, dst, device, cond))

    def arrive(self, index, slot, device, cond=None):
        self.run(cond, lambda: self.copy(index, slot, slot, device).wait_recv())

    def finish(self):
        for index, src, dst, device, cond in self.started:
            self.run(cond, lambda: self.copy(index, src, dst, device).wait_send())


def greet(pairs):
    barrier = pltpu.get_barrier_semaphore()
    for device, cond in pairs:
        def hello(device=device):
            pl.semaphore_signal(barrier, inc=1, device_id=device, device_id_type=MESH)

        if cond is None:
            hello()
        else:
            pl.when(cond)(hello)
    peers = sum(1 if cond is None else cond.astype(jnp.int32) for _, cond in pairs)
    pl.semaphore_wait(barrier, peers)


class RowGather:
    def __init__(self, block, out, send_sem, recv_sem):
        row, col = lax.axis_index("row"), lax.axis_index("col")
        self.row = row
        self.z, self.y = row // YN, lax.rem(row, YN)
        self.block, self.out = block, out
        self.up = (row + YN, col)
        self.down = (row - YN, col)
        self.has_up = self.z < ZL - 1
        self.has_down = self.z > 0
        self.after = (self.z * YN + lax.rem(self.y + 1, YN), col)
        self.before = (self.z * YN + lax.rem(self.y + YN - 1, YN), col)
        self.net = Sender(send_sem, recv_sem)

    def partners(self):
        return [
            (self.up, self.has_up),
            (self.down, self.has_down),
            (self.after, None),
            (self.before, None),
        ]

    def slot(self, z, shift):
        return lambda: self.out(z * YN + lax.rem(self.y + shift + YN, YN))

    def events(self, distance):
        events = [(0, self.z - distance, self.z - distance >= 0)]
        if distance > 0:
            events.append((1, self.z + distance, self.z + distance < ZL))
        return events

    def along_z(self, distance):
        for way, z, exists in self.events(distance):
            mine = self.slot(z, 0)
            src = mine
            if distance == 0:
                src = lambda: self.block
            else:
                self.net.arrive(way * 8 + distance, mine, self.down if way == 0 else self.up, exists)
            if distance < ZL - 1:
                if way == 0:
                    self.net.send(
                        distance + 1, src, mine, self.up, jnp.logical_and(exists, self.has_up)
                    )
                if way == 1 or distance == 0:
                    self.net.send(
                        8 + distance + 1, src, mine, self.down, jnp.logical_and(exists, self.has_down)
                    )
            cond = None if distance == 0 else exists
            self.net.send(16 + way * 8 + distance, src, mine, self.after, cond)
            self.net.send(32 + way * 8 + distance, src, mine, self.before, cond)

    def along_y(self, distance):
        for way, z, exists in self.events(distance):
            cond = None if distance == 0 else exists
            index = way * 8 + distance
            self.net.arrive(16 + index, self.slot(z, -1), self.before, cond)
            if distance % 2 == 0:
                self.net.send(48 + index, self.slot(z, -1), self.slot(z, -1), self.after, cond)
            self.net.arrive(32 + index, self.slot(z, 1), self.after, cond)
            if distance % 2 == 1:
                self.net.send(48 + index, self.slot(z, 1), self.slot(z, 1), self.before, cond)

    def last(self):
        for distance in range(ZL):
            for way, z, exists in self.events(distance):
                cond = None if distance == 0 else exists
                source = self.before if distance % 2 == 0 else self.after
                self.net.arrive(48 + way * 8 + distance, self.slot(z, 2), source, cond)
        self.net.finish()


class Halves:
    def __init__(self, block, out, sems):
        part = block.shape[0] // 2
        self.halves = [
            RowGather(
                block.at[pl.ds(which * part, part)],
                lambda index, first=which * part: out.at[index, pl.ds(first, part)],
                sems[2 * which],
                sems[2 * which + 1],
            )
            for which in range(2)
        ]
        self.row = self.halves[0].row

    def partners(self):
        return self.halves[0].partners()

    def along_z(self, distance):
        for half in self.halves:
            half.along_z(distance)

    def along_y(self, distance):
        for half in self.halves:
            half.along_y(distance)

    def last(self):
        for half in self.halves:
            half.last()


class ColGather:
    def __init__(self, block, out, send_sem, recv_sem):
        row, col = lax.axis_index("row"), lax.axis_index("col")
        self.high, self.x, self.core = col // (2 * XN), lax.rem(col // 2, XN), lax.rem(col, 2)
        self.block, self.out = block, out
        self.mate = (row, self.at(1, 0, 0))
        self.after = (row, self.at(0, 1, 0))
        self.before = (row, self.at(0, -1, 0))
        self.sibling = (row, self.at(0, 0, 1))
        self.net = Sender(send_sem, recv_sem)

    def partners(self):
        return [(self.mate, None), (self.after, None), (self.before, None), (self.sibling, None)]

    def at(self, high, shift, core):
        return (
            lax.rem(self.high + high, 2) * (2 * XN)
            + lax.rem(self.x + shift + XN, XN) * 2
            + lax.rem(self.core + core, 2)
        )

    def slot(self, high, shift, core=0):
        return lambda: self.out.at[self.at(high, shift, core)]

    def own(self, high):
        slot = self.slot(high, 0)
        src = slot
        if high == 0:
            src = lambda: self.block
            self.net.send(0, src, slot, self.mate)
        else:
            self.net.arrive(0, slot, self.mate)
        self.net.send(1 + high, src, slot, self.after)
        self.net.send(3 + high, src, slot, self.before)
        self.net.send(8 + high * 4, src, slot, self.sibling)

    def ring(self, high):
        self.net.arrive(1 + high, self.slot(high, -1), self.before)
        if high == 0:
            self.net.send(5, self.slot(high, -1), self.slot(high, -1), self.after)
        self.net.send(8 + high * 4 + 3, self.slot(high, -1), self.slot(high, -1), self.sibling)
        self.net.arrive(3 + high, self.slot(high, 1), self.after)
        if high == 1:
            self.net.send(6, self.slot(high, 1), self.slot(high, 1), self.before)
        self.net.send(8 + high * 4 + 1, self.slot(high, 1), self.slot(high, 1), self.sibling)

    def far(self, high):
        self.net.arrive(5 + high, self.slot(high, 2), self.before if high == 0 else self.after)
        self.net.send(8 + high * 4 + 2, self.slot(high, 2), self.slot(high, 2), self.sibling)

    def last(self):
        for high in range(2):
            for shift in range(XN):
                self.net.arrive(8 + high * 4 + shift, self.slot(high, shift, 1), self.sibling)
        self.net.finish()


def project(all_weight, hidden, query_ref, kv_ref, query_sum, kv_sum):
    query_sum[...] = jnp.zeros_like(query_sum)
    kv_sum[...] = jnp.zeros_like(kv_sum)

    @pl.loop(0, 4 * XN)
    def _(block):
        def columns(first):
            return jnp.concatenate(
                [
                    all_weight[2 * block, pl.ds(first, PIECE), :],
                    all_weight[2 * block + 1, pl.ds(first, PIECE), :],
                ],
                axis=0,
            )

        mine = hidden[block]
        for half in range(2):
            query_sum[:, pl.ds(half * 128, 128)] += jnp.dot(
                mine, columns(Q_AT + half * PIECE), preferred_element_type=jnp.float32
            )
        kv_sum[...] += jnp.dot(mine, columns(KV_AT), preferred_element_type=jnp.float32)

    query_ref[...] = query_sum[...].astype(jnp.bfloat16)
    kv_ref[...] = kv_sum[...].astype(jnp.bfloat16)


def normalise(all_token, gain_ref, hidden, squares):
    squares[...] = jnp.zeros_like(squares)

    @pl.loop(0, 4 * XN)
    def _(block):
        wide = all_token[block].astype(jnp.float32)
        squares[...] += wide * wide

    tail = squares[TOK:]
    tail = jnp.concatenate(
        [
            jnp.sum(tail[:, :64], axis=1, keepdims=True),
            jnp.sum(tail[:, 64:], axis=1, keepdims=True),
        ],
        axis=0,
    )
    mean = (jnp.sum(squares[:TOK], axis=1, keepdims=True) + tail) * (1.0 / WIDTH)
    inverse = lax.rsqrt(mean + 1e-05)

    @pl.loop(0, 4 * XN)
    def _(block):
        rows = unfold(all_token[block].astype(jnp.float32))
        hidden[block] = (rows * inverse * gain_ref[block]).astype(jnp.bfloat16)


def gather_kernel(
    weight_ref, token_ref, gain_ref, all_weight, query_ref, kv_ref, all_token, hidden, squares,
    query_sum, kv_sum, rs, rr, rs2, rr2, cs, cr, local_sem,
):
    rows = Halves(weight_ref, all_weight, (rs, rr, rs2, rr2))
    cols = ColGather(token_ref, all_token, cs, cr)
    greet(rows.partners() + cols.partners())
    cols.own(0)
    rows.along_z(0)
    own_weight = pltpu.make_async_copy(weight_ref, all_weight.at[rows.row], local_sem.at[0])
    own_token = pltpu.make_async_copy(
        token_ref, all_token.at[lax.axis_index("col")], local_sem.at[1]
    )
    own_weight.start()
    own_token.start()
    rows.along_z(1)
    rows.along_y(0)
    cols.ring(0)
    rows.along_z(2)
    rows.along_y(1)
    cols.own(1)
    rows.along_z(3)
    rows.along_y(2)
    cols.far(0)
    rows.along_z(4)
    rows.along_y(3)
    cols.ring(1)
    rows.along_z(5)
    rows.along_y(4)
    cols.far(1)
    rows.along_z(6)
    rows.along_y(5)
    rows.along_z(7)
    rows.along_y(6)
    cols.last()
    own_token.wait()
    normalise(all_token, gain_ref, hidden, squares)
    rows.along_y(7)
    rows.last()
    own_weight.wait()
    project(all_weight, hidden, query_ref, kv_ref, query_sum, kv_sum)


def vmem():
    return pl.BlockSpec(memory_space=pltpu.VMEM)


def gather_first(weight_block, token_block, gain):
    return pl.pallas_call(
        gather_kernel,
        out_shape=(
            jax.ShapeDtypeStruct((ZL * YN,) + weight_block.shape, jnp.bfloat16),
            jax.ShapeDtypeStruct((TOK, 256), jnp.bfloat16),
            jax.ShapeDtypeStruct((TOK, 128), jnp.bfloat16),
        ),
        in_specs=[vmem()] * 3,
        out_specs=(vmem(),) * 3,
        scratch_shapes=[
            pltpu.VMEM((4 * XN, FOLD, 128), jnp.bfloat16),
            pltpu.VMEM((4 * XN, TOK, FEAT), jnp.bfloat16),
            pltpu.VMEM((FOLD, 128), jnp.float32),
            pltpu.VMEM((TOK, 256), jnp.float32),
            pltpu.VMEM((TOK, 128), jnp.float32),
            pltpu.SemaphoreType.DMA((ROW_COPIES,)),
            pltpu.SemaphoreType.DMA((ROW_COPIES,)),
            pltpu.SemaphoreType.DMA((ROW_COPIES,)),
            pltpu.SemaphoreType.DMA((ROW_COPIES,)),
            pltpu.SemaphoreType.DMA((COL_COPIES,)),
            pltpu.SemaphoreType.DMA((COL_COPIES,)),
            pltpu.SemaphoreType.DMA((2,)),
        ],
        compiler_params=pltpu.CompilerParams(
            collective_id=0, has_side_effects=True, vmem_limit_bytes=40 * 1024 * 1024
        ),
    )(weight_block, token_block, gain)


def kv_kernel(block_ref, out_ref, rs, rr, rs2, rr2, local_sem):
    rows = Halves(block_ref, out_ref, (rs, rr, rs2, rr2))
    greet(rows.partners())
    rows.along_z(0)
    own = pltpu.make_async_copy(block_ref, out_ref.at[rows.row], local_sem.at[0])
    own.start()
    for distance in range(1, ZL):
        rows.along_z(distance)
        rows.along_y(distance - 1)
    rows.along_y(ZL - 1)
    rows.last()
    own.wait()


def gather_kv(block):
    return pl.pallas_call(
        kv_kernel,
        out_shape=jax.ShapeDtypeStruct((ZL * YN,) + block.shape, jnp.bfloat16),
        in_specs=[vmem()],
        out_specs=vmem(),
        scratch_shapes=[
            pltpu.SemaphoreType.DMA((ROW_COPIES,)),
            pltpu.SemaphoreType.DMA((ROW_COPIES,)),
            pltpu.SemaphoreType.DMA((ROW_COPIES,)),
            pltpu.SemaphoreType.DMA((ROW_COPIES,)),
            pltpu.SemaphoreType.DMA((1,)),
        ],
        compiler_params=pltpu.CompilerParams(
            collective_id=1, has_side_effects=True, vmem_limit_bytes=40 * 1024 * 1024
        ),
    )(block)


ORDER = ((1, 2), (0, 2), (1, 1), (1, 3), (0, 3), (0, 1), (1, 0), (0, 0))


def out_kernel(
    att_ref, weight_ref, token_ref, out_ref, first, landed, second, ring, keep, mate_out, mate_in,
    send_sem, recv_sem,
):
    row, col = lax.axis_index("row"), lax.axis_index("col")
    high, x, core = col // (2 * XN), lax.rem(col // 2, XN), lax.rem(col, 2)

    def at(dh, dx, dc):
        return (
            lax.rem(high + dh, 2) * (2 * XN) + lax.rem(x + dx + XN, XN) * 2 + lax.rem(core + dc, 2)
        )

    mate, after, before, sibling = (
        (row, at(1, 0, 0)), (row, at(0, 1, 0)), (row, at(0, -1, 0)), (row, at(0, 0, 1)),
    )
    greet([(mate, None), (after, None), (before, None), (sibling, None)])
    net = Sender(send_sem, recv_sem)

    def share(block):
        product = jnp.zeros((TOK, FEAT), jnp.float32)
        for half in range(2):
            columns = jnp.concatenate(
                [
                    weight_ref[2 * block + piece, pl.ds(O_AT + half * PIECE, PIECE), :]
                    for piece in range(2)
                ],
                axis=0,
            )
            product += lax.dot_general(
                att_ref[:, pl.ds(half * 128, 128)],
                columns,
                (((1,), (1,)), ((), ())),
                preferred_element_type=jnp.float32,
            )
        return fold(product)

    for k, (dh, dx) in enumerate(ORDER):
        first[k] = share(at(dh, dx, 1)).astype(jnp.bfloat16)
        net.send(k, lambda k=k: first.at[k], lambda k=k: landed.at[k], sibling)

    def summed(k):
        dh, dx = ORDER[k]
        own = share(at(dh, dx, 0))
        net.arrive(k, lambda: landed.at[k], sibling)
        return own + landed[k].astype(jnp.float32)

    def pass_on(index, value, device):
        second[index] = value.astype(jnp.bfloat16)
        net.send(8 + index, lambda: second.at[index], lambda: ring.at[index], device)

    def arrived(index, device):
        net.arrive(8 + index, lambda: ring.at[index], device)
        return ring[index].astype(jnp.float32)

    pass_on(0, summed(0), before)
    pass_on(1, summed(1), after)
    pass_on(2, summed(2), after)
    keep[0] = summed(3)
    pass_on(4, keep[0] + arrived(0, after), before)
    pass_on(3, summed(4), before)
    keep[1] = summed(5)
    pass_on(5, keep[1] + arrived(1, before), after)
    keep[2] = summed(6)
    mate_out[...] = (keep[2] + arrived(2, before) + arrived(4, after)).astype(jnp.bfloat16)
    net.send(14, lambda: mate_out, lambda: mate_in, mate)
    keep[3] = summed(7) + token_ref[...].astype(jnp.float32)
    total = keep[3] + arrived(3, after) + arrived(5, before)
    net.arrive(14, lambda: mate_in, mate)
    out_ref[...] = (total + mate_in[...].astype(jnp.float32)).astype(jnp.bfloat16)
    net.finish()


def project_out(att, weights, tokens):
    block = (FOLD, 128)
    return pl.pallas_call(
        out_kernel,
        out_shape=jax.ShapeDtypeStruct(block, jnp.bfloat16),
        in_specs=[vmem()] * 3,
        out_specs=vmem(),
        scratch_shapes=[
            pltpu.VMEM((8,) + block, jnp.bfloat16),
            pltpu.VMEM((8,) + block, jnp.bfloat16),
            pltpu.VMEM((6,) + block, jnp.bfloat16),
            pltpu.VMEM((6,) + block, jnp.bfloat16),
            pltpu.VMEM((4,) + block, jnp.float32),
            pltpu.VMEM(block, jnp.bfloat16),
            pltpu.VMEM(block, jnp.bfloat16),
            pltpu.SemaphoreType.DMA((16,)),
            pltpu.SemaphoreType.DMA((16,)),
        ],
        compiler_params=pltpu.CompilerParams(
            collective_id=2, has_side_effects=True, vmem_limit_bytes=40 * 1024 * 1024
        ),
    )(att, weights, tokens)


def body(
    prefill_hidden,
    decode_hidden,
    norm_gain,
    query_weight,
    kv_weight,
    out_weight,
    sink_logits,
    key_pool,
    value_pool,
    lengths,
    page_table,
):
    spans, span_rows, col_width = prefill_hidden.shape
    decode_rows = decode_hidden.shape[0]
    heads = query_weight.shape[1] // HD
    col_index = lax.axis_index("col")
    row_index = lax.axis_index("row")
    kv_head = col_index * heads // (HQ // KV)
    half_rows = (spans // 2) * span_rows
    gap = HALF - half_rows - decode_rows

    def padded(array, axis):
        pads = [(0, 0)] * array.ndim
        pads[axis] = (0, PIECE - array.shape[axis])
        return jnp.pad(array, pads)

    def two_halves(prefill, decode):
        wide = prefill.shape[1]
        return jnp.concatenate(
            [
                prefill[:half_rows],
                decode,
                jnp.zeros((gap, wide), decode.dtype),
                prefill[half_rows:],
                jnp.zeros((HALF - half_rows, wide), decode.dtype),
            ],
            axis=0,
        )

    kv_mine = padded(
        jnp.concatenate(
            [
                lax.dynamic_slice_in_dim(kv_weight[:, which], kv_head * HD, HD, 1)
                for which in range(2)
            ],
            axis=1,
        ),
        0,
    )
    query_mine = padded(query_weight, 0)
    out_mine = padded(out_weight.T, 0)
    weight_block = jnp.concatenate(
        [
            query_mine[:, :128],
            query_mine[:, 128:],
            out_mine[:, :128],
            out_mine[:, 128:],
            kv_mine,
        ],
        axis=0,
    )
    part = col_width // 2
    token_rows = two_halves(prefill_hidden.reshape(-1, col_width), decode_hidden)
    token_block = fold(
        jnp.concatenate(
            [padded(token_rows[:, :part], 1), padded(token_rows[:, part:], 1)], axis=1
        )
    )
    gain = (
        padded(norm_gain.astype(jnp.float32).reshape(-1, part), 1).reshape(4 * XN, 1, FEAT)
    )
    all_weight, queries, kv_rows = gather_first(weight_block, token_block, gain)
    kv_all = (
        gather_kv(jnp.concatenate([kv_rows[:half_rows], kv_rows[HALF : HALF + half_rows]], axis=0))
        .reshape(-1, spans, span_rows, 2 * HD)
        .transpose(1, 0, 2, 3)
        .reshape(spans, -1, 2 * HD)
    )
    score_scale = 1.0 / math.sqrt(HD)
    sink = sink_logits.astype(jnp.float32)
    query_pre = jnp.concatenate(
        [queries[:half_rows], queries[HALF : HALF + half_rows]], axis=0
    ).reshape(spans, span_rows, heads, HD)
    key_pair, value_pair = kv_all[..., :HD], kv_all[..., HD:]
    positions = row_index * span_rows + jnp.arange(span_rows, dtype=jnp.int32)
    scores = (
        jnp.einsum("sqgd,spd->sgqp", query_pre, key_pair, preferred_element_type=jnp.float32)
        * score_scale
    )
    key_pos = jnp.arange(key_pair.shape[1], dtype=jnp.int32)
    scores = jnp.where(key_pos[None, :] <= positions[:, None], scores, -jnp.inf)
    sink_pre = sink[None, :, None]
    highest = jnp.maximum(jnp.max(scores, axis=-1), sink_pre)
    probs = jnp.exp(scores - highest[..., None])
    denominator = jnp.sum(probs, axis=-1) + jnp.exp(sink_pre - highest)
    weighted = jnp.einsum(
        "sgqp,spd->sgqd",
        probs.astype(jnp.bfloat16),
        value_pair,
        preferred_element_type=jnp.float32,
    )
    prefill_att = (
        (weighted / denominator[..., None])
        .transpose(0, 2, 1, 3)
        .reshape(spans * span_rows, heads * HD)
        .astype(jnp.bfloat16)
    )
    query_dec = queries[half_rows : half_rows + decode_rows].reshape(decode_rows, heads, HD)
    new_rows = kv_rows[half_rows : half_rows + decode_rows]
    key_new, value_new = new_rows[:, :HD], new_rows[:, HD:]
    table = page_table.reshape(decode_rows, -1)
    page_len = key_pool.shape[1]
    key_mine = lax.dynamic_slice_in_dim(key_pool, kv_head * HD, HD, 2)
    value_mine = lax.dynamic_slice_in_dim(value_pool, kv_head * HD, HD, 2)
    cached = table.shape[1] * page_len
    key_cache = key_mine[table].reshape(decode_rows, cached, HD)
    value_cache = value_mine[table].reshape(decode_rows, cached, HD)
    cache_scores = (
        jnp.einsum("sgd,std->sgt", query_dec, key_cache, preferred_element_type=jnp.float32)
        * score_scale
    )
    live = jnp.arange(cached, dtype=jnp.int32)[None, :] < lengths.reshape(decode_rows)[:, None]
    cache_scores = jnp.where(live[:, None, :], cache_scores, -jnp.inf)
    self_scores = (
        jnp.einsum("sgd,sd->sg", query_dec, key_new, preferred_element_type=jnp.float32)
        * score_scale
    )
    highest = jnp.maximum(jnp.maximum(jnp.max(cache_scores, axis=-1), self_scores), sink[None])
    cache_probs = jnp.exp(cache_scores - highest[..., None])
    self_probs = jnp.exp(self_scores - highest)
    denom_dec = jnp.sum(cache_probs, axis=-1) + self_probs + jnp.exp(sink[None] - highest)
    decode_sum = jnp.einsum(
        "sgt,std->sgd",
        cache_probs.astype(jnp.bfloat16),
        value_cache,
        preferred_element_type=jnp.float32,
    )
    decode_sum = (
        decode_sum
        + self_probs.astype(jnp.bfloat16).astype(jnp.float32)[..., None]
        * value_new.astype(jnp.float32)[:, None, :]
    )
    decode_att = (
        (decode_sum / denom_dec[..., None]).reshape(decode_rows, heads * HD).astype(jnp.bfloat16)
    )
    result = unfold(project_out(two_halves(prefill_att, decode_att), all_weight, token_block))
    result = jnp.concatenate([result[:, :part], result[:, PIECE : PIECE + part]], axis=1)
    prefill_out = jnp.concatenate([result[:half_rows], result[HALF : HALF + half_rows]], axis=0)
    return (
        prefill_out.reshape(spans, span_rows, col_width),
        result[half_rows : half_rows + decode_rows],
    )


def solution(mesh):
    in_specs = (
        P(None, "row", "col"),
        P("row", "col"),
        P(),
        P("row", "col"),
        P("row", None, None),
        P("col", "row"),
        P("col"),
        P("row", None, None),
        P("row", None, None),
        P("row", None),
        P("row", None),
    )
    out_specs = (P(None, "row", "col"), P("row", "col"))
    return jax.shard_map(body, mesh=mesh, in_specs=in_specs, out_specs=out_specs, check_vma=False)
```
